256 devices in a mesh: dp: 2 (over core), row: 16 (over y, x), col: 8 (over z).
Axes of the slice: x: 4, y: 4, z: 8, core: 2. Of those that a mesh axis runs over, the one named last changes fastest.
Arguments:
- features: bfloat16 [256, 96, 2048], P(('dp', 'row'), 'col'), parts along dimension 0, may hold values from 0 to 40
- low_level: bfloat16 [512, 192, 256], P(('dp', 'row'), 'col'), parts along dimension 0, may hold values from -6 to 6
- point_weight: bfloat16 [2048, 256], P(None, 'row'), may hold values from -0.125 to 0.125
- atrous_weight: bfloat16 [3, 3, 3, 2048, 256], P(None, None, None, None, 'row'), may hold values from -0.046875 to 0.046875
- pool_weight: bfloat16 [2048, 256], P(None, 'row'), may hold values from -0.125 to 0.125
- aspp_bias: float32 [5, 256], P(None, 'row'), may hold values from -1.5 to 1.5
- proj_weight: bfloat16 [1280, 256], replicated, may hold values from -0.15625 to 0.15625
- proj_bias: float32 [256], replicated, may hold values from -1.5 to 1.5
- low_weight: bfloat16 [256, 48], replicated, may hold values from -0.375 to 0.375
- low_bias: float32 [48], replicated, may hold values from -1.5 to 1.5
- conv1_weight: bfloat16 [3, 3, 304, 256], replicated, may hold values from -0.109375 to 0.109375
- conv1_bias: float32 [256], replicated, may hold values from -1.5 to 1.5
- conv2_weight: bfloat16 [3, 3, 256, 256], replicated, may hold values from -0.125 to 0.125
- conv2_bias: float32 [256], replicated, may hold values from -1.5 to 1.5
Outputs:
- decoded: bfloat16 [512, 192, 256], P(('dp', 'row'), 'col'), parts along dimension 0
The draws below stay inside these ranges and needn't reach their ends.
There are 2 independent parts, one for each index of `dp`. The reference program is written for one: setup_inputs(seed, part) draws one part's arguments, and reference() takes and returns one part's arrays. A program takes and returns all parts, laid end to end along the dimension named above; an argument that names none is the same for every part. Nothing has to cross between parts.
All inputs are finite; a program needn't handle non-finite values.
Results may differ from the reference program's by a relative error of at most 0.0057.
Values may be sent and summed in bfloat16 or wider, within the bound.
No kernel may reach another device: no remote copies, remote signals or barrier semaphores. Data moves between devices by JAX's collectives and lax.ppermute only.
A program may use at most 128 MiB of HBM per device.

```python
import jax
import jax.numpy as jnp

C_IN = 2048
C_ASPP = 256
C_LOW = 256
C_RED = 48
C_DEC = 256
TR = 8
TC = 12
MAP_H = 128
MAP_W = 96


def smooth_profile(coeff_key, length):
    coefficients = jax.random.uniform(coeff_key, (2, C_IN), jnp.float32, -1.0, 1.0)
    position = 2.0 * jnp.arange(length, dtype=jnp.float32) / max(length - 1, 1) - 1.0
    linear_part = 0.5 * coefficients[0][None, :] * position[:, None]
    curved_part = 0.3 * coefficients[1][None, :] * (position[:, None] * position[:, None] - 1.0 / 3.0)
    return 1.0 + linear_part + curved_part


def draw_features(key, part):
    base_key, chan_key, level_key, row_key, col_key = jax.random.split(jax.random.fold_in(key, 11), 5)
    shape = (MAP_H, MAP_W, C_IN)
    channel_scale = jnp.exp(jax.random.uniform(chan_key, (C_IN,), jnp.float32, jnp.log(0.3), jnp.log(3.0)))
    row_trend = 1.0 + 2.0 * jnp.arange(MAP_H, dtype=jnp.float32) / max(MAP_H - 1, 1)
    tile_levels = jnp.exp(jax.random.uniform(level_key, (MAP_H // TR, MAP_W // TC), jnp.float32, jnp.log(0.6), jnp.log(1.4)))
    level_map = jnp.repeat(jnp.repeat(tile_levels, TR, axis=0), TC, axis=1)
    row_profile = smooth_profile(row_key, MAP_H)
    col_profile = smooth_profile(col_key, MAP_W)
    base_values = jnp.minimum(jnp.abs(jax.random.normal(base_key, shape, jnp.float32)) / 3.0, 1.0)
    values = base_values * channel_scale[None, None, :] * row_trend[:, None, None]
    values = values * level_map[:, :, None] * row_profile[:, None, :] * col_profile[None, :, :]
    return values.astype(jnp.bfloat16)


def shard_levels(key, shape, shards, low, largest):
    def one(dim, parts):
        draws = jax.random.uniform(jax.random.fold_in(jax.random.fold_in(key, 6), dim), (parts,), jnp.float32, low / len(shards), largest / len(shards))
        return jnp.repeat(jnp.exp(draws), shape[dim] // parts).reshape((-1,) + (1,) * (len(shape) - dim - 1))

    factor_of = one(*shards[0])
    for cut in shards[1:]:
        factor_of = factor_of * one(*cut)
    return factor_of


def scatter_about(stream_key, shape, scale, reach, shards=(), held_as=jnp.bfloat16):
    values = scale * jax.random.normal(stream_key, shape, jnp.float32)
    if shards:
        values = values * shard_levels(stream_key, shape, shards, -0.22, 0.18)
    return jnp.clip(values, -reach, reach).astype(held_as)


def setup_inputs(seed: int = 0, part: int = 0) -> dict:
    streams_of = jax.random.split(jax.random.key(seed), 15)
    part_keys = jax.random.split(jax.random.fold_in(streams_of[14], part), 15)
    features = draw_features(jax.random.fold_in(jax.random.fold_in(streams_of[14], part), 71), part)
    low_level = scatter_about(part_keys[1], (2 * MAP_H, 2 * MAP_W, C_LOW), 1.0, 6.0, ((0, 16), (1, 8)))
    point_weight = scatter_about(streams_of[2], (C_IN, C_ASPP), C_IN ** -0.5, 0.125, ((1, 16),))
    atrous_weight = scatter_about(streams_of[3], (3, 3, 3, C_IN, C_ASPP), (9 * C_IN) ** -0.5, 0.046875, ((4, 16),))
    pool_weight = scatter_about(streams_of[4], (C_IN, C_ASPP), C_IN ** -0.5, 0.125, ((1, 16),))
    aspp_bias = scatter_about(streams_of[5], (5, C_ASPP), 0.3, 1.5, ((1, 16),), jnp.float32)
    proj_weight = scatter_about(streams_of[6], (5 * C_ASPP, C_ASPP), (5 * C_ASPP) ** -0.5, 0.15625)
    proj_bias = scatter_about(streams_of[7], (C_ASPP,), 0.3, 1.5, (), jnp.float32)
    low_weight = scatter_about(streams_of[8], (C_LOW, C_RED), C_LOW ** -0.5, 0.375)
    low_bias = scatter_about(streams_of[9], (C_RED,), 0.3, 1.5, (), jnp.float32)
    conv1_weight = scatter_about(streams_of[10], (3, 3, C_ASPP + C_RED, C_DEC), (9 * (C_ASPP + C_RED)) ** -0.5, 0.109375)
    conv1_bias = scatter_about(streams_of[11], (C_DEC,), 0.3, 1.5, (), jnp.float32)
    conv2_weight = scatter_about(streams_of[12], (3, 3, C_DEC, C_DEC), (9 * C_DEC) ** -0.5, 0.125)
    conv2_bias = scatter_about(streams_of[13], (C_DEC,), 0.3, 1.5, (), jnp.float32)
    return dict(features=features, low_level=low_level, point_weight=point_weight, atrous_weight=atrous_weight, pool_weight=pool_weight, aspp_bias=aspp_bias, proj_weight=proj_weight, proj_bias=proj_bias, low_weight=low_weight, low_bias=low_bias, conv1_weight=conv1_weight, conv1_bias=conv1_bias, conv2_weight=conv2_weight, conv2_bias=conv2_bias)


RATES = (12, 24, 36)


def shifted(field, row_off, col_off):
    height, width = field.shape[0], field.shape[1]
    extent = max(abs(row_off), abs(col_off))
    padded = jnp.pad(field, ((extent, extent), (extent, extent), (0, 0)))
    return padded[extent + row_off:extent + row_off + height, extent + col_off:extent + col_off + width]


def enlarge(padded):
    values = padded.astype(jnp.float32)
    middle = values[1:-1]
    even = 0.75 * middle + 0.25 * values[:-2]
    odd = 0.75 * middle + 0.25 * values[2:]
    values = jnp.stack([even, odd], axis=1).reshape(2 * middle.shape[0], middle.shape[1], middle.shape[2])
    middle = values[:, 1:-1]
    even = 0.75 * middle + 0.25 * values[:, :-2]
    odd = 0.75 * middle + 0.25 * values[:, 2:]
    values = jnp.stack([even, odd], axis=2).reshape(values.shape[0], 2 * middle.shape[1], middle.shape[2])
    return values.astype(jnp.bfloat16)


def convolve(padded, weight, bias):
    height, width = padded.shape[0] - 2, padded.shape[1] - 2
    windows = []
    for row_tap in range(3):
        for col_tap in range(3):
            windows.append(padded[row_tap:row_tap + height, col_tap:col_tap + width])
    columns = jnp.concatenate(windows, axis=2)
    depth = columns.shape[2]
    result = jnp.dot(columns.reshape(-1, depth), weight.reshape(depth, -1), preferred_element_type=jnp.float32)
    result = jnp.maximum(result + bias, 0.0).astype(jnp.bfloat16)
    return result.reshape(height, width, -1)


def reference(features, low_level, point_weight, atrous_weight, pool_weight, aspp_bias, proj_weight, proj_bias, low_weight, low_bias, conv1_weight, conv1_bias, conv2_weight, conv2_bias):
    height, width = features.shape[0], features.shape[1]
    flat_rows = features.reshape(-1, features.shape[2])

    def activate(values, number):
        return jnp.maximum(values + aspp_bias[number], 0.0).astype(jnp.bfloat16)

    outputs = [activate(jnp.dot(flat_rows, point_weight, preferred_element_type=jnp.float32).reshape(height, width, -1), 0)]
    for rate_number in range(3):
        dilation = RATES[rate_number]
        running = jnp.zeros((height, width, point_weight.shape[1]), jnp.float32)
        for row_tap in range(3):
            for col_tap in range(3):
                term = jnp.dot(flat_rows, atrous_weight[rate_number, row_tap, col_tap], preferred_element_type=jnp.float32)
                running = running + shifted(term.reshape(height, width, -1), (row_tap - 1) * dilation, (col_tap - 1) * dilation)
        outputs.append(activate(running, rate_number + 1))
    pooled = jnp.sum(jnp.dot(flat_rows, pool_weight, preferred_element_type=jnp.float32), axis=0) / (height * width)
    pool_branch = jnp.maximum(pooled + aspp_bias[4], 0.0).astype(jnp.bfloat16)
    outputs.append(jnp.broadcast_to(pool_branch, (height, width, pool_branch.shape[0])))
    joined = jnp.concatenate(outputs, axis=2)
    coarse = jnp.dot(joined.reshape(height * width, -1), proj_weight, preferred_element_type=jnp.float32)
    coarse = jnp.maximum(coarse + proj_bias, 0.0).astype(jnp.bfloat16).reshape(height, width, -1)
    upsampled = enlarge(jnp.pad(coarse, ((1, 1), (1, 1), (0, 0)), mode="edge"))
    low_rows = low_level.reshape(-1, low_level.shape[2])
    reduced = jnp.dot(low_rows, low_weight, preferred_element_type=jnp.float32)
    reduced = jnp.maximum(reduced + low_bias, 0.0).astype(jnp.bfloat16).reshape(2 * height, 2 * width, -1)
    joined_fine = jnp.concatenate([upsampled, reduced], axis=2)
    hidden = convolve(jnp.pad(joined_fine, ((1, 1), (1, 1), (0, 0))), conv1_weight, conv1_bias)
    return convolve(jnp.pad(hidden, ((1, 1), (1, 1), (0, 0))), conv2_weight, conv2_bias)
```

```python
import jax
import jax.numpy as jnp
from jax import lax
from jax.experimental import pallas as pl
from jax.experimental.pallas import tpu as pltpu
from jax.sharding import Mesh
from jax.sharding import PartitionSpec as P

ROW = ("row_0", "row_1")
DP_ROW = ("dp", "row_0", "row_1")
RATES = (12, 24, 36)
MAP_ROWS = 128
MAP_COLS = 96
BF = jnp.bfloat16
F32 = jnp.float32
VMEM_BYTES = 56 * 1024 * 1024


def around(value, axis, by):
    devices = lax.axis_size(axis)
    return lax.ppermute(value, axis, [(i, (i + by) % devices) for i in range(devices)])


def next_to(value, axis, by):
    devices = lax.axis_size(axis)
    pairs = [(i, i + by) for i in range(devices) if 0 <= i + by < devices]
    return lax.ppermute(value, axis, pairs)


def gather_strip(half, first, second):
    behind = around(half, first, 1)
    ahead = around(half, first, -1)
    far_low = around(behind[:3], first, 1)
    far_high = around(ahead[3:], first, -1)
    line = jnp.concatenate([half, behind, ahead, far_low, far_high], axis=0)
    line_behind = around(line, second, 1)
    line_ahead = around(line, second, -1)
    far_behind = around(line_behind[:12], second, 1)
    far_ahead = around(line_ahead[12:], second, -1)
    return [line, line_behind, line_ahead, far_behind, far_ahead]


LINE = ((0, 6, 0, 0), (6, 6, 0, -1), (12, 6, 0, 1), (18, 3, 0, 2), (21, 3, 3, 2))
PIECES = (
    [(0, *piece, 0) for piece in LINE]
    + [(1, *piece, -1) for piece in LINE]
    + [(2, *piece, 1) for piece in LINE]
    + [(3, *piece, 2) for piece in LINE[:2]]
    + [(4, start - 12, count, col, step, 2) for start, count, col, step in LINE[2:]]
)


def products_kernel(*refs):
    place = refs[0]
    parts = (refs[1:6], refs[6:11])
    atrous, point, pool = refs[11:14]
    centre = refs[14]
    sides = refs[15:21]
    pooled = refs[21]
    feats, weights, total, feat_sems, weight_sems = refs[22:27]
    own_y, own_x = place[0], place[1]
    copies = []
    for colour in range(2):
        group = []
        for number, (which, start, count, col, first, second) in enumerate(PIECES):
            step_y, step_x = (second, first) if colour == 0 else (first, second)
            tile = ((own_y + step_y + 4) % 4) * 4 + (own_x + step_x + 4) % 4
            group.append(
                pltpu.make_async_copy(
                    parts[colour][which].at[pl.ds(start, count)],
                    feats.at[pl.ds(6 * colour + col, count), tile],
                    feat_sems.at[colour * len(PIECES) + number],
                )
            )
        copies.append(group)
    loads = [
        pltpu.make_async_copy(atrous, weights.at[pl.ds(0, 432)], weight_sems.at[0]),
        pltpu.make_async_copy(point, weights.at[pl.ds(432, 16)], weight_sems.at[1]),
        pltpu.make_async_copy(pool, weights.at[pl.ds(448, 16)], weight_sems.at[2]),
    ]
    for copy in loads + copies[0] + copies[1]:
        copy.start()
    total[...] = jnp.zeros_like(total)
    lane = lax.broadcasted_iota(jnp.int32, (16, MAP_ROWS), 1)

    def shifted(value, offset):
        if offset == 0:
            return value
        moved = pltpu.roll(value, (-offset) % MAP_ROWS, 1)
        inside = (lane + offset >= 0) & (lane + offset < MAP_ROWS)
        return jnp.where(inside, moved, 0.0)

    def pair(index, carry):
        block = feats[pl.ds(2 * index, 2)].reshape(2 * MAP_ROWS, feats.shape[-1])
        result = lax.dot_general(
            weights[...], block, (((1,), (1,)), ((), ())), preferred_element_type=F32
        )
        for side in range(2):
            col = 2 * index + side
            columns = result[:, side * MAP_ROWS : (side + 1) * MAP_ROWS]

            def group(number, columns=columns):
                return columns[number * 16 : (number + 1) * 16]

            centre[col, 0:16] = group(27)
            for rate in range(3):
                for col_tap in range(3):
                    summed = group(rate * 9 + 3 + col_tap)
                    summed = summed + shifted(group(rate * 9 + col_tap), -RATES[rate])
                    summed = summed + shifted(group(rate * 9 + 6 + col_tap), RATES[rate])
                    if col_tap == 1:
                        centre[col, 16 * (rate + 1) : 16 * (rate + 2)] = summed
                    else:
                        sides[2 * rate + col_tap // 2][col] = summed.astype(BF)
            total[...] += group(28)
        return carry

    for copy in loads + copies[0]:
        copy.wait()
    lax.fori_loop(0, 3, pair, 0)
    for copy in copies[1]:
        copy.wait()
    lax.fori_loop(3, 6, pair, 0)
    strip = jnp.sum(total[...], axis=1, keepdims=True)
    high = strip.astype(BF).astype(F32)
    middle = (strip - high).astype(BF).astype(F32)
    low = strip - high - middle
    terms = jnp.where(lane == 0, high, jnp.where(lane == 1, middle, jnp.where(lane == 2, low, 0.0)))
    terms = terms.astype(BF)
    for side in sides:
        side[12] = terms
    pooled[...] = terms


def products(place, pieces, atrous, point, pool):
    depth = atrous.shape[1]
    side = jax.ShapeDtypeStruct((13, 16, MAP_ROWS), BF)
    anywhere = pl.BlockSpec(memory_space=pl.ANY)
    return pl.pallas_call(
        products_kernel,
        out_shape=[jax.ShapeDtypeStruct((12, 64, MAP_ROWS), F32)]
        + [side] * 6
        + [jax.ShapeDtypeStruct((16, MAP_ROWS), BF)],
        in_specs=[pl.BlockSpec(memory_space=pltpu.SMEM)] + [anywhere] * 13,
        scratch_shapes=[
            pltpu.VMEM((12, 16, 8, depth), BF),
            pltpu.VMEM((464, depth), BF),
            pltpu.VMEM((16, MAP_ROWS), F32),
            pltpu.SemaphoreType.DMA((2 * len(PIECES),)),
            pltpu.SemaphoreType.DMA((3,)),
        ],
        compiler_params=pltpu.CompilerParams(vmem_limit_bytes=VMEM_BYTES),
        name="products",
    )(place, *pieces, atrous, point, pool)


def branches_kernel(place, centre, *refs):
    sides = refs[0:6]
    pooled, opposite, bias, out, rows, slots = refs[6:12]
    strip = place[2]
    for c6 in range(6):
        halves = []
        for half in range(2):
            col = half * 6 + c6
            values = [centre[col, 0:16] + bias[0:16]]
            for rate in range(3):
                running = centre[col, 16 * (rate + 1) : 16 * (rate + 2)]
                for tap in range(2):
                    source = strip + (rate + 1) * (2 * tap - 1)
                    inside = (source >= 0) & (source < 8)
                    running = running + jnp.where(
                        inside, sides[2 * rate + tap][col].astype(F32), 0.0
                    )
                values.append(running + bias[16 * (rate + 1) : 16 * (rate + 2)])
            halves.extend(values)
        block = jnp.maximum(jnp.concatenate(halves, axis=0), 0.0)
        rows[c6, 0:8] = jnp.zeros((8, 128), F32)
        rows[c6, 8:136] = block.T
        rows[c6, 136:144] = jnp.zeros((8, 128), F32)
    terms = pooled[...].astype(F32) + opposite[...].astype(F32)
    for side in sides:
        terms = terms + side[12].astype(F32)
    mean = jnp.sum(terms, axis=1, keepdims=True) / (MAP_ROWS * MAP_COLS)
    branch = jnp.maximum(mean + bias[64:80], 0.0)
    wide = jnp.concatenate(
        [jnp.broadcast_to(branch, (16, 128)), jnp.zeros((112, 128), F32)], axis=0
    ).T
    for slot in range(16):
        for c6 in range(6):
            slots[slot, c6 * 12 : c6 * 12 + 12] = rows[c6, 8 * slot + 6 : 8 * slot + 18]
        slots[slot, 72:80] = wide[0:8]
        out[slot] = slots[slot].astype(BF)


def branches(place, centre, sides, pooled, opposite, bias):
    smem = pl.BlockSpec(memory_space=pltpu.SMEM)
    vmem = pl.BlockSpec(memory_space=pltpu.VMEM)
    return pl.pallas_call(
        branches_kernel,
        out_shape=jax.ShapeDtypeStruct((16, 80, 128), BF),
        in_specs=[smem] + [vmem] * 10,
        scratch_shapes=[pltpu.VMEM((6, 144, 128), F32), pltpu.VMEM((16, 80, 128), F32)],
        compiler_params=pltpu.CompilerParams(vmem_limit_bytes=VMEM_BYTES),
        name="branches",
    )(place, centre, *sides, pooled, opposite, bias)


def project_kernel(received, weight, pool_weight, bias, out, first, last):
    lane = lax.broadcasted_iota(jnp.int32, (80, 128), 1)
    blocks = [received[source].astype(F32) for source in range(16)]
    turned = [pltpu.roll(block, 64, 1) for block in blocks]
    halves = []
    for half in range(2):
        pieces = []
        for source in range(0, 16, 2):
            left = blocks[source] if half == 0 else turned[source]
            right = turned[source + 1] if half == 0 else blocks[source + 1]
            pieces.append(jnp.where(lane < 64, left, right)[0:72])
        halves.append(jnp.concatenate(pieces, axis=1))
    stacked = jnp.concatenate(halves, axis=0).astype(BF)
    low = blocks[0][72:80]
    high = blocks[8][72:80]
    for source in range(1, 8):
        low = low + pltpu.roll(blocks[source][72:80], 16 * source, 1)
        high = high + pltpu.roll(blocks[source + 8][72:80], 16 * source, 1)
    vector = jnp.concatenate([low, high], axis=1).astype(BF)
    constant = jnp.dot(vector, pool_weight[...], preferred_element_type=F32)[0:1]
    summed = jnp.dot(stacked, weight[...], preferred_element_type=F32)
    coarse = jnp.maximum(summed + constant + bias[...], 0.0).astype(BF)
    out[...] = coarse
    first[...] = coarse[0:24]
    last[...] = coarse[120:144]


def project(received, weight, pool_weight, bias):
    return pl.pallas_call(
        project_kernel,
        out_shape=[
            jax.ShapeDtypeStruct((144, 256), BF),
            jax.ShapeDtypeStruct((24, 256), BF),
            jax.ShapeDtypeStruct((24, 256), BF),
        ],
        compiler_params=pltpu.CompilerParams(vmem_limit_bytes=VMEM_BYTES),
        name="project",
    )(received, weight, pool_weight, bias)


def decode_kernel(
    place, before, coarse, after, spread, low, w1, b1, w2, b2, out, fine, fine_cols, mid, mid_cols
):
    wide = jnp.concatenate([before[...], coarse[...], after[...]], axis=0)
    fine[0:640] = jnp.dot(spread[...], wide, preferred_element_type=F32)
    fine[640:656] = jnp.zeros((16, 256), F32)
    for tap in range(3):
        fine_cols[tap] = fine[tap : tap + 640].astype(BF)
    acc = jnp.zeros((576, 256), F32)
    for row_tap in range(3):
        rows = slice(row_tap * 32, row_tap * 32 + 576)
        for tap in range(3):
            acc = acc + jnp.dot(
                fine_cols[tap, rows], w1[row_tap, tap, 0:256], preferred_element_type=F32
            )
        small = jnp.concatenate([w1[row_tap, tap, 256:304] for tap in range(3)], axis=0)
        acc = acc + jnp.dot(low[rows], small, preferred_element_type=F32)
    position = lax.broadcasted_iota(jnp.int32, (576, 256), 0)
    y = 16 * (place[0] * 4 + place[1]) - 1 + (position >> 5)
    x = 24 * place[2] - 1 + (position & 31)
    inside = (y >= 0) & (y < 2 * MAP_ROWS) & (x >= 0) & (x < 2 * MAP_COLS)
    mid[0:576] = jnp.where(inside, jnp.maximum(acc + b1[...], 0.0), 0.0)
    mid[576:592] = jnp.zeros((16, 256), F32)
    for tap in range(3):
        mid_cols[tap] = mid[tap : tap + 576].astype(BF)
    acc = jnp.zeros((512, 256), F32)
    for row_tap in range(3):
        for tap in range(3):
            acc = acc + jnp.dot(
                mid_cols[tap, row_tap * 32 : row_tap * 32 + 512],
                w2[row_tap, tap],
                preferred_element_type=F32,
            )
    result = jnp.maximum(acc + b2[...], 0.0).astype(BF).reshape(16, 32, 256)
    out[...] = result[:, 0:24]


def decode(place, before, coarse, after, spread, low, w1, b1, w2, b2):
    smem = pl.BlockSpec(memory_space=pltpu.SMEM)
    vmem = pl.BlockSpec(memory_space=pltpu.VMEM)
    return pl.pallas_call(
        decode_kernel,
        out_shape=jax.ShapeDtypeStruct((16, 24, 256), BF),
        in_specs=[smem] + [vmem] * 9,
        scratch_shapes=[
            pltpu.VMEM((656, 256), F32),
            pltpu.VMEM((3, 640, 256), BF),
            pltpu.VMEM((592, 256), F32),
            pltpu.VMEM((3, 576, 256), BF),
        ],
        compiler_params=pltpu.CompilerParams(vmem_limit_bytes=VMEM_BYTES),
        name="decode",
    )(place, before, coarse, after, spread, low, w1, b1, w2, b2)


def spread_matrix(row_index, col_index):
    n = lax.broadcasted_iota(jnp.int32, (640, 192), 0)
    m = lax.broadcasted_iota(jnp.int32, (640, 192), 1)

    def weights(fine, size, coarse):
        near = fine >> 1
        other = jnp.where((fine & 1) == 1, near + 1, near - 1)
        other = jnp.clip(other, 0, size - 1)
        value = jnp.where(coarse == near, 0.75, 0.0) + jnp.where(coarse == other, 0.25, 0.0)
        return jnp.where((fine >= 0) & (fine < 2 * size), value, 0.0)

    rows = weights(16 * row_index - 2 + (n >> 5), MAP_ROWS, 8 * row_index - 2 + m % 12)
    cols = weights(24 * col_index - 2 + (n & 31), MAP_COLS, 12 * col_index - 2 + m // 12)
    return (rows * cols).astype(BF)


def low_columns(low_level, weight, bias):
    reduced = jnp.dot(
        low_level.reshape(-1, low_level.shape[2]), weight, preferred_element_type=F32
    )
    reduced = jnp.maximum(reduced + bias, 0.0).astype(BF).reshape(16, 24, -1)
    above = next_to(reduced[14:16], ROW, 1)
    below = next_to(reduced[0:2], ROW, -1)
    tall = jnp.concatenate([above, reduced, below], axis=0)
    before = next_to(tall[:, 22:24], "col", 1)
    after = next_to(tall[:, 0:2], "col", -1)
    full = jnp.concatenate([before, tall, after], axis=1)
    full = jnp.pad(full, ((0, 1), (0, 4), (0, 0))).reshape(672, -1)
    return jnp.concatenate([full[tap : tap + 640] for tap in range(3)], axis=1)


def on_device(
    features,
    low_level,
    point_weight,
    atrous_weight,
    pool_weight,
    aspp_bias,
    proj_weight,
    proj_bias,
    low_weight,
    low_bias,
    conv1_weight,
    conv1_bias,
    conv2_weight,
    conv2_bias,
):
    in_width = features.shape[2]
    own_y, own_x = lax.axis_index("row_0"), lax.axis_index("row_1")
    row_index, col_index = lax.axis_index(ROW), lax.axis_index("col")
    place = jnp.stack([own_y, own_x, col_index]).astype(jnp.int32)
    tile = jnp.transpose(features, (1, 0, 2))
    pieces = gather_strip(tile[:6], "row_1", "row_0") + gather_strip(tile[6:], "row_0", "row_1")
    low = low_columns(low_level, low_weight, low_bias)
    spread = spread_matrix(row_index, col_index)
    atrous = jnp.transpose(atrous_weight, (0, 1, 2, 4, 3)).reshape(432, in_width)
    centre, *sides, pooled = products(place, pieces, atrous, point_weight.T, pool_weight.T)
    moved = [None] * 6
    for rate in (2, 1, 0):
        moved[2 * rate] = around(sides[2 * rate], "col", rate + 1)
        moved[2 * rate + 1] = around(sides[2 * rate + 1], "col", -rate - 1)
    opposite = around(pooled, "col", 4)
    mine = branches(place, centre, moved, pooled, opposite, aspp_bias.reshape(80, 1))
    received = lax.all_to_all(mine, ROW, split_axis=0, concat_axis=0, tiled=True)
    blocks = proj_weight.reshape(5, 16, 16, 256)
    ordered = jnp.transpose(blocks[:4], (1, 0, 2, 3)).reshape(1024, 256)
    coarse, first, last = project(received, ordered, proj_weight[1024:], proj_bias.reshape(1, 256))
    before = next_to(last, "col", 1)
    after = next_to(first, "col", -1)
    return decode(
        place,
        before,
        coarse,
        after,
        spread,
        low,
        conv1_weight,
        conv1_bias.reshape(1, 256),
        conv2_weight,
        conv2_bias.reshape(1, 256),
    )


def solution(mesh):
    torus = Mesh(
        mesh.devices.reshape(mesh.shape["dp"], 4, 4, mesh.shape["col"]),
        ("dp", "row_0", "row_1", "col"),
    )
    placed = (
        P(DP_ROW, "col", None),
        P(DP_ROW, "col", None),
        P(None, ROW),
        P(None, None, None, None, ROW),
        P(None, ROW),
        P(None, ROW),
        P(),
        P(),
        P(),
        P(),
        P(),
        P(),
        P(),
        P(),
    )
    return jax.shard_map(
        on_device, mesh=torus, in_specs=placed, out_specs=P(DP_ROW, "col", None), check_vma=False
    )
```

```python
import jax
import jax.numpy as jnp
from jax import lax
from jax.experimental import pallas as pl
from jax.experimental.pallas import tpu as pltpu
from jax.sharding import Mesh
from jax.sharding import PartitionSpec as P

ROW = ("row_0", "row_1")
DP_ROW = ("dp", "row_0", "row_1")
RATES = (12, 24, 36)
MAP_ROWS = 128
MAP_COLS = 96
BF = jnp.bfloat16
F32 = jnp.float32
VMEM_BYTES = 56 * 1024 * 1024


def around(value, axis, by):
    devices = lax.axis_size(axis)
    return lax.ppermute(value, axis, [(i, (i + by) % devices) for i in range(devices)])


def next_to(value, axis, by):
    devices = lax.axis_size(axis)
    pairs = [(i, i + by) for i in range(devices) if 0 <= i + by < devices]
    return lax.ppermute(value, axis, pairs)


def swap(value, axis, near):
    pairs = ((0, 1), (2, 3)) if near else ((0, 3), (1, 2))
    return lax.ppermute(value, axis, [way for a, b in pairs for way in ((a, b), (b, a))])


OWN, NEAR, WRAP, FAR = range(4)


def position(index, kind):
    if kind == OWN:
        return index
    if kind == NEAR:
        return index + 1 - 2 * (index % 2)
    if kind == WRAP:
        return 3 - index
    return (index + 2) % 4


def gather_strip(half, first, second):
    near = swap(half, first, True)
    wrap = swap(half, first, False)
    far_low = swap(near[:3], first, False)
    far_high = swap(wrap[3:], first, True)
    low = jnp.concatenate([half, near], axis=0)
    high = jnp.concatenate([wrap, far_low, far_high], axis=0)
    low_near = swap(low, second, True)
    low_wrap = swap(low, second, False)
    high_wrap = swap(high, second, False)
    high_near = swap(high, second, True)
    low_far = swap(low_near, second, False)
    high_far = swap(high_wrap, second, True)
    return [low, high, low_near, high_near, low_wrap, high_wrap, low_far, high_far]


LOW = ((0, 6, 0, OWN), (6, 6, 0, NEAR))
HIGH = ((0, 6, 0, WRAP), (6, 3, 0, FAR), (9, 3, 3, FAR))
PIECES = [
    (2 * which + part, *piece, kind)
    for which, kind in enumerate((OWN, NEAR, WRAP, FAR))
    for part, pieces in enumerate((LOW, HIGH))
    for piece in pieces
]
SIZES = (23, 17, 15)


def products_kernel(*refs):
    refs = (None, *refs)
    parts = (refs[1:9], refs[9:17])
    atrous, point, pool = refs[17:20]
    centre = refs[20]
    sides = refs[21:27]
    opposite = refs[27]
    feats, weights, total, feat_sems, weight_sems = refs[28:33]
    own_y, own_x = lax.axis_index("row_0"), lax.axis_index("row_1")
    copies = []
    for colour in range(2):
        group = []
        for number, (which, start, count, col, first, second) in enumerate(PIECES):
            kind_y, kind_x = (second, first) if colour == 0 else (first, second)
            tile = position(own_y, kind_y) * 4 + position(own_x, kind_x)
            group.append(
                pltpu.make_async_copy(
                    parts[colour][which].at[pl.ds(start, count)],
                    feats.at[pl.ds(6 * colour + col, count), tile],
                    feat_sems.at[colour * len(PIECES) + number],
                )
            )
        copies.append(group)
    loads = [
        pltpu.make_async_copy(atrous, weights.at[pl.ds(0, 432)], weight_sems.at[0]),
        pltpu.make_async_copy(point, weights.at[pl.ds(432, 16)], weight_sems.at[1]),
        pltpu.make_async_copy(pool, weights.at[pl.ds(448, 16)], weight_sems.at[2]),
    ]
    for copy in loads + copies[0] + copies[1]:
        copy.start()
    total[...] = jnp.zeros_like(total)
    lane = lax.broadcasted_iota(jnp.int32, (16, MAP_ROWS), 1)

    def shifted(value, offset):
        if offset == 0:
            return value
        moved = pltpu.roll(value, (-offset) % MAP_ROWS, 1)
        inside = (lane + offset >= 0) & (lane + offset < MAP_ROWS)
        return jnp.where(inside, moved, 0.0)

    def pair(index, carry):
        block = feats[pl.ds(2 * index, 2)].reshape(2 * MAP_ROWS, feats.shape[-1])
        result = lax.dot_general(
            weights[...], block, (((1,), (1,)), ((), ())), preferred_element_type=F32
        )
        for side in range(2):
            col = 2 * index + side
            columns = result[:, side * MAP_ROWS : (side + 1) * MAP_ROWS]

            def group(number, columns=columns):
                return columns[number * 16 : (number + 1) * 16]

            centre[col, 0:16] = group(27)
            for rate in range(3):
                for col_tap in range(3):
                    summed = group(rate * 9 + 3 + col_tap)
                    summed = summed + shifted(group(rate * 9 + col_tap), -RATES[rate])
                    summed = summed + shifted(group(rate * 9 + 6 + col_tap), RATES[rate])
                    if col_tap == 1:
                        centre[col, 16 * (rate + 1) : 16 * (rate + 2)] = summed
                    else:
                        sides[2 * rate + col_tap // 2][col] = summed.astype(BF)
            total[...] += group(28)
        return carry

    for copy in loads + copies[0]:
        copy.wait()
    lax.fori_loop(0, 3, pair, 0)
    for copy in copies[1]:
        copy.wait()
    lax.fori_loop(3, 6, pair, 0)
    strip = jnp.sum(total[...], axis=1, keepdims=True)
    high = strip.astype(BF).astype(F32)
    middle = (strip - high).astype(BF).astype(F32)
    low = strip - high - middle
    terms = jnp.where(lane == 0, high, jnp.where(lane == 1, middle, jnp.where(lane == 2, low, 0.0)))
    terms = terms.astype(BF)
    for rate in range(3):
        for way in range(2):
            sides[2 * rate + way][SIZES[rate] - 1] = terms
    opposite[4] = terms
    for edge in range(2):
        for way in range(2):
            near, middle_rate, far = sides[way], sides[2 + way], sides[4 + way]
            here, there = (edge, 10 + edge) if way == 0 else (10 + edge, edge)
            for branch in range(4):
                piece = centre[there, 16 * branch : 16 * (branch + 1)]
                near[12 + 2 * branch + edge] = piece.astype(BF)
            near[20 + edge] = middle_rate[here]
            middle_rate[12 + edge] = near[there]
            middle_rate[14 + edge] = far[here]
            far[12 + edge] = middle_rate[there]
            opposite[2 - 2 * way + edge] = far[there]


def products(pieces, atrous, point, pool):
    depth = atrous.shape[1]
    sides = [jax.ShapeDtypeStruct((size, 16, MAP_ROWS), BF) for size in SIZES for _ in range(2)]
    anywhere = pl.BlockSpec(memory_space=pl.ANY)
    return pl.pallas_call(
        products_kernel,
        out_shape=[jax.ShapeDtypeStruct((12, 64, MAP_ROWS), F32)]
        + sides
        + [jax.ShapeDtypeStruct((5, 16, MAP_ROWS), BF)],
        in_specs=[anywhere] * 19,
        scratch_shapes=[
            pltpu.VMEM((12, 16, 8, depth), BF),
            pltpu.VMEM((464, depth), BF),
            pltpu.VMEM((16, MAP_ROWS), F32),
            pltpu.SemaphoreType.DMA((2 * len(PIECES),)),
            pltpu.SemaphoreType.DMA((3,)),
        ],
        compiler_params=pltpu.CompilerParams(vmem_limit_bytes=VMEM_BYTES),
        name="products",
    )(*pieces, atrous, point, pool)


def branches_kernel(centre, *refs):
    sides = refs[0:6]
    opposite, own_left, own_right, own_terms, bias, out, rows, slots = refs[6:14]
    strip = lax.axis_index("col")

    diagonal = lax.broadcasted_iota(jnp.int32, (16, 16), 0) == lax.broadcasted_iota(
        jnp.int32, (16, 16), 1
    )

    def bias_column(branch):
        row = jnp.broadcast_to(bias[branch : branch + 1], (16, 16))
        return jnp.sum(jnp.where(diagonal, row, 0.0), axis=1, keepdims=True)

    def brought(distance, index):
        ref = opposite
        if abs(distance) < 4:
            ref = sides[2 * (abs(distance) - 1) + (1 if distance > 0 else 0)]
        source = strip + distance
        inside = (source >= 0) & (source < 8)
        return jnp.where(inside, ref[index].astype(F32), 0.0)

    def column(c16):
        if 2 <= c16 < 14:
            col = c16 - 2
            values = [centre[col, 0:16]]
            for rate in range(3):
                running = centre[col, 16 * (rate + 1) : 16 * (rate + 2)]
                values.append(running + brought(-rate - 1, col) + brought(rate + 1, col))
            return values
        edge = c16 % 2
        side = -1 if c16 < 2 else 1
        own = own_right[10 + edge] if side < 0 else own_left[edge]
        values = [brought(side, 12 + 2 * branch + edge) for branch in range(4)]
        last = 2 + edge if side < 0 else edge
        values[1] = values[1] + brought(2 * side, 12 + edge) + own.astype(F32)
        values[2] = values[2] + brought(3 * side, 12 + edge) + brought(-side, 20 + edge)
        values[3] = values[3] + brought(4 * side, last) + brought(-2 * side, 14 + edge)
        return values

    for c8 in range(8):
        values = column(c8) + column(c8 + 8)
        biases = [bias_column(k % 4) for k in range(8)]
        block = jnp.concatenate([v + b for v, b in zip(values, biases)], axis=0)
        rows[c8, 0:8] = jnp.zeros((8, 128), F32)
        rows[c8, 8:136] = jnp.maximum(block, 0.0).T
        rows[c8, 136:144] = jnp.zeros((8, 128), F32)
    terms = own_terms[4].astype(F32) + opposite[4].astype(F32)
    for rate in range(3):
        for way in range(2):
            terms = terms + sides[2 * rate + way][SIZES[rate] - 1].astype(F32)
    mean = jnp.sum(terms, axis=1, keepdims=True) / (MAP_ROWS * MAP_COLS)
    branch = jnp.maximum(mean + bias_column(4), 0.0)
    wide = jnp.concatenate(
        [jnp.broadcast_to(branch, (16, 128)), jnp.zeros((112, 128), F32)], axis=0
    ).T
    for slot in range(16):
        for c8 in range(8):
            slots[slot, c8 * 12 : c8 * 12 + 12] = rows[c8, 8 * slot + 6 : 8 * slot + 18]
        slots[slot, 96:104] = wide[0:8]
        out[slot] = slots[slot].astype(BF)


def branches(centre, moved, opposite, own_left, own_right, own_terms, bias):
    vmem = pl.BlockSpec(memory_space=pltpu.VMEM)
    return pl.pallas_call(
        branches_kernel,
        out_shape=jax.ShapeDtypeStruct((16, 104, 128), BF),
        in_specs=[vmem] * 12,
        scratch_shapes=[pltpu.VMEM((8, 144, 128), F32), pltpu.VMEM((16, 104, 128), F32)],
        compiler_params=pltpu.CompilerParams(vmem_limit_bytes=VMEM_BYTES),
        name="branches",
    )(centre, *moved, opposite, own_left, own_right, own_terms, bias)


def coarse_tile(received, weight, pool_weight, bias):
    lane = lax.broadcasted_iota(jnp.int32, (104, 128), 1)
    blocks = [received[source].astype(F32) for source in range(16)]
    turned = [pltpu.roll(block, 64, 1) for block in blocks]
    halves = []
    for half in range(2):
        pieces = []
        for source in range(0, 16, 2):
            left = blocks[source] if half == 0 else turned[source]
            right = turned[source + 1] if half == 0 else blocks[source + 1]
            pieces.append(jnp.where(lane < 64, left, right)[0:96])
        halves.append(jnp.concatenate(pieces, axis=1))
    stacked = jnp.concatenate(halves, axis=0).astype(BF)
    low = blocks[0][96:104]
    high = blocks[8][96:104]
    for source in range(1, 8):
        low = low + pltpu.roll(blocks[source][96:104], 16 * source, 1)
        high = high + pltpu.roll(blocks[source + 8][96:104], 16 * source, 1)
    vector = jnp.concatenate([low, high], axis=1).astype(BF)
    constant = jnp.dot(vector, pool_weight, preferred_element_type=F32)[0:1]
    summed = jnp.dot(stacked, weight, preferred_element_type=F32)
    return jnp.maximum(summed + constant + bias[...], 0.0).astype(BF)


def decode_kernel(*refs):
    received, proj, bias, spread, low, w1_hbm, b1, w2_hbm, b2 = refs[0:9]
    out, fine, fine_cols, mid, mid_cols, w1, w2, weight, last, sems = refs[9:]
    loads = [
        pltpu.make_async_copy(w1_hbm, w1, sems.at[0]),
        pltpu.make_async_copy(w2_hbm, w2, sems.at[1]),
    ]
    small_loads = [
        pltpu.make_async_copy(proj.at[branch], weight.at[:, branch], sems.at[2 + branch])
        for branch in range(4)
    ]
    small_loads.append(pltpu.make_async_copy(proj.at[4], last, sems.at[6]))
    for load in small_loads + loads:
        load.start()
    for load in small_loads:
        load.wait()
    coarse = coarse_tile(
        received, weight[...].reshape(1024, 256), last[...].reshape(256, 256), bias
    )
    fine[0:640] = jnp.dot(spread[...], coarse, preferred_element_type=F32)
    fine[640:656] = jnp.zeros((16, 256), F32)
    for tap in range(3):
        fine_cols[tap] = fine[tap : tap + 640].astype(BF)
    loads[0].wait()
    acc = jnp.zeros((576, 256), F32)
    for row_tap in range(3):
        rows = slice(row_tap * 32, row_tap * 32 + 576)
        for tap in range(3):
            acc = acc + jnp.dot(
                fine_cols[tap, rows], w1[row_tap, tap, 0:256], preferred_element_type=F32
            )
        small = jnp.concatenate([w1[row_tap, tap, 256:304] for tap in range(3)], axis=0)
        acc = acc + jnp.dot(low[rows], small, preferred_element_type=F32)
    at = lax.broadcasted_iota(jnp.int32, (576, 256), 0)
    y = 16 * (lax.axis_index("row_0") * 4 + lax.axis_index("row_1")) - 1 + (at >> 5)
    x = 24 * lax.axis_index("col") - 1 + (at & 31)
    inside = (y >= 0) & (y < 2 * MAP_ROWS) & (x >= 0) & (x < 2 * MAP_COLS)
    mid[0:576] = jnp.where(inside, jnp.maximum(acc + b1[...], 0.0), 0.0)
    mid[576:592] = jnp.zeros((16, 256), F32)
    for tap in range(3):
        mid_cols[tap] = mid[tap : tap + 576].astype(BF)
    loads[1].wait()
    acc = jnp.zeros((512, 256), F32)
    for row_tap in range(3):
        for tap in range(3):
            acc = acc + jnp.dot(
                mid_cols[tap, row_tap * 32 : row_tap * 32 + 512],
                w2[row_tap, tap],
                preferred_element_type=F32,
            )
    result = jnp.maximum(acc + b2[...], 0.0).astype(BF).reshape(16, 32, 256)
    out[...] = result[:, 0:24]


def decode(received, proj, bias, spread, low, w1, b1, w2, b2):
    vmem = pl.BlockSpec(memory_space=pltpu.VMEM)
    hbm = pl.BlockSpec(memory_space=pl.ANY)
    return pl.pallas_call(
        decode_kernel,
        out_shape=jax.ShapeDtypeStruct((16, 24, 256), BF),
        in_specs=[vmem, hbm, vmem, vmem, vmem, hbm, vmem, hbm, vmem],
        scratch_shapes=[
            pltpu.VMEM((656, 256), F32),
            pltpu.VMEM((3, 640, 256), BF),
            pltpu.VMEM((592, 256), F32),
            pltpu.VMEM((3, 576, 256), BF),
            pltpu.VMEM(w1.shape, BF),
            pltpu.VMEM(w2.shape, BF),
            pltpu.VMEM((16, 4, 16, 256), BF),
            pltpu.VMEM((16, 16, 256), BF),
            pltpu.SemaphoreType.DMA((7,)),
        ],
        compiler_params=pltpu.CompilerParams(vmem_limit_bytes=VMEM_BYTES),
        name="decode",
    )(received, proj, bias, spread, low, w1, b1, w2, b2)


def spread_kernel(out):
    n = lax.broadcasted_iota(jnp.int32, (640, 192), 0)
    m = lax.broadcasted_iota(jnp.int32, (640, 192), 1)
    col = (m * 683) >> 13
    row_index = lax.axis_index("row_0") * 4 + lax.axis_index("row_1")
    strip = lax.axis_index("col")

    def weights(fine, size, coarse):
        near = fine >> 1
        other = jnp.where((fine & 1) == 1, near + 1, near - 1)
        other = jnp.clip(other, 0, size - 1)
        value = jnp.where(coarse == near, 0.75, 0.0) + jnp.where(coarse == other, 0.25, 0.0)
        return jnp.where((fine >= 0) & (fine < 2 * size), value, 0.0)

    rows = weights(16 * row_index - 2 + (n >> 5), MAP_ROWS, 8 * row_index - 2 + m - 12 * col)
    cols = weights(24 * strip - 2 + (n & 31), MAP_COLS, 12 * strip - 2 + col)
    out[...] = (rows * cols).astype(BF)


def spread_matrix():
    return pl.pallas_call(
        spread_kernel,
        out_shape=jax.ShapeDtypeStruct((640, 192), BF),
        name="spread",
    )()


def reduce_low(low_level, weight, bias):
    reduced = jnp.dot(
        low_level.reshape(-1, low_level.shape[2]), weight, preferred_element_type=F32
    )
    reduced = jnp.maximum(reduced + bias, 0.0).astype(BF).reshape(16, 24, -1)
    return reduced


def low_columns(above, wide, below):
    full = jnp.concatenate([above, wide, below], axis=0)
    full = jnp.pad(full, ((0, 1), (0, 4), (0, 0))).reshape(672, -1)
    return jnp.concatenate([full[tap : tap + 640] for tap in range(3)], axis=1)


def on_device(
    features,
    low_level,
    point_weight,
    atrous_weight,
    pool_weight,
    aspp_bias,
    proj_weight,
    proj_bias,
    low_weight,
    low_bias,
    conv1_weight,
    conv1_bias,
    conv2_weight,
    conv2_bias,
):
    in_width = features.shape[2]
    tile = jnp.transpose(features, (1, 0, 2))
    reduced = reduce_low(low_level, low_weight, low_bias)
    before = next_to(reduced[:, 22:24], "col", 1)
    after = next_to(reduced[:, 0:2], "col", -1)
    wide = jnp.concatenate([before, reduced, after], axis=1)
    above = next_to(wide[14:16], ROW, 1)
    below = next_to(wide[0:2], ROW, -1)
    low = low_columns(above, wide, below)
    pieces = gather_strip(tile[:6], "row_1", "row_0")
    pieces += gather_strip(tile[6:], "row_0", "row_1")
    spread = spread_matrix()
    atrous = jnp.transpose(atrous_weight, (0, 1, 2, 4, 3)).reshape(432, in_width)
    centre, *sides, opposite = products(pieces, atrous, point_weight.T, pool_weight.T)
    moved = []
    for rate in range(3):
        moved.append(around(sides[2 * rate], "col", rate + 1))
        moved.append(around(sides[2 * rate + 1], "col", -rate - 1))
    across = around(opposite, "col", 4)
    mine = branches(centre, moved, across, sides[0], sides[1], opposite, aspp_bias)
    received = lax.all_to_all(mine, ROW, split_axis=0, concat_axis=0, tiled=True)
    return decode(
        received,
        proj_weight.reshape(5, 16, 16, 256),
        proj_bias.reshape(1, 256),
        spread,
        low,
        conv1_weight,
        conv1_bias.reshape(1, 256),
        conv2_weight,
        conv2_bias.reshape(1, 256),
    )


def solution(mesh):
    torus = Mesh(
        mesh.devices.reshape(mesh.shape["dp"], 4, 4, mesh.shape["col"]),
        ("dp", "row_0", "row_1", "col"),
    )
    placed = (
        P(DP_ROW, "col", None),
        P(DP_ROW, "col", None),
        P(None, ROW),
        P(None, None, None, None, ROW),
        P(None, ROW),
        P(None, ROW),
        P(),
        P(),
        P(),
        P(),
        P(),
        P(),
        P(),
        P(),
    )
    return jax.shard_map(
        on_device, mesh=torus, in_specs=placed, out_specs=P(DP_ROW, "col", None), check_vma=False
    )
```

```python
import jax
import jax.numpy as jnp
from jax import lax
from jax.experimental import pallas as pl
from jax.experimental.pallas import tpu as pltpu
from jax.sharding import Mesh
from jax.sharding import PartitionSpec as P

ROW = ("row_0", "row_1")
DP_ROW = ("dp", "row_0", "row_1")
RATES = (12, 24, 36)
MAP_ROWS = 128
MAP_COLS = 96
BF = jnp.bfloat16
F32 = jnp.float32
VMEM_BYTES = 56 * 1024 * 1024


def around(value, axis, by):
    devices = lax.axis_size(axis)
    return lax.ppermute(value, axis, [(i, (i + by) % devices) for i in range(devices)])


def next_to(value, axis, by):
    devices = lax.axis_size(axis)
    pairs = [(i, i + by) for i in range(devices) if 0 <= i + by < devices]
    return lax.ppermute(value, axis, pairs)


def swap(value, axis, near):
    pairs = ((0, 1), (2, 3)) if near else ((0, 3), (1, 2))
    return lax.ppermute(value, axis, [way for a, b in pairs for way in ((a, b), (b, a))])


OWN, NEAR, WRAP, FAR = range(4)


def position(index, kind):
    if kind == OWN:
        return index
    if kind == NEAR:
        return index + 1 - 2 * (index % 2)
    if kind == WRAP:
        return 3 - index
    return (index + 2) % 4


def gather_strip(half, first, second):
    near = swap(half, first, True)
    wrap = swap(half, first, False)
    far_low = swap(near[:3], first, False)
    far_high = swap(wrap[3:], first, True)
    low = jnp.concatenate([half, near], axis=0)
    high = jnp.concatenate([wrap, far_low, far_high], axis=0)
    low_near = swap(low, second, True)
    low_wrap = swap(low, second, False)
    high_wrap = swap(high, second, False)
    high_near = swap(high, second, True)
    low_far = swap(low_near, second, False)
    high_far = swap(high_wrap, second, True)
    return [low, high, low_near, high_near, low_wrap, high_wrap, low_far, high_far]


LOW = ((0, 6, 0, OWN), (6, 6, 0, NEAR))
HIGH = ((0, 6, 0, WRAP), (6, 3, 0, FAR), (9, 3, 3, FAR))
PIECES = [
    (2 * which + part, *piece, kind)
    for which, kind in enumerate((OWN, NEAR, WRAP, FAR))
    for part, pieces in enumerate((LOW, HIGH))
    for piece in pieces
]
SIZES = (23, 17, 15)
SLOT = 136


def products_kernel(*refs):
    refs = (None, *refs)
    parts = (refs[1:9], refs[9:17])
    atrous, point, pool = refs[17:20]
    centre = refs[20]
    sides = refs[21:27]
    opposite = refs[27]
    feats, weights, total, feat_sems, weight_sems = refs[28:33]
    own_y, own_x = lax.axis_index("row_0"), lax.axis_index("row_1")
    copies = []
    for colour in range(2):
        group = []
        for number, (which, start, count, col, first, second) in enumerate(PIECES):
            kind_y, kind_x = (second, first) if colour == 0 else (first, second)
            tile = position(own_y, kind_y) * 4 + position(own_x, kind_x)
            group.append(
                pltpu.make_async_copy(
                    parts[colour][which].at[pl.ds(start, count)],
                    feats.at[pl.ds(6 * colour + col, count), tile],
                    feat_sems.at[colour * len(PIECES) + number],
                )
            )
        copies.append(group)
    loads = [
        pltpu.make_async_copy(atrous, weights.at[pl.ds(0, 432)], weight_sems.at[0]),
        pltpu.make_async_copy(point, weights.at[pl.ds(432, 16)], weight_sems.at[1]),
        pltpu.make_async_copy(pool, weights.at[pl.ds(448, 16)], weight_sems.at[2]),
    ]
    for copy in loads + copies[0] + copies[1]:
        copy.start()
    total[...] = jnp.zeros_like(total)
    lane = lax.broadcasted_iota(jnp.int32, (16, MAP_ROWS), 1)

    def shifted(value, offset):
        if offset == 0:
            return value
        moved = pltpu.roll(value, (-offset) % MAP_ROWS, 1)
        inside = (lane + offset >= 0) & (lane + offset < MAP_ROWS)
        return jnp.where(inside, moved, 0.0)

    def pair(index, carry):
        block = feats[pl.ds(2 * index, 2)].reshape(2 * MAP_ROWS, feats.shape[-1])
        result = lax.dot_general(
            weights[...], block, (((1,), (1,)), ((), ())), preferred_element_type=F32
        )
        for side in range(2):
            col = 2 * index + side
            columns = result[:, side * MAP_ROWS : (side + 1) * MAP_ROWS]

            def group(number, columns=columns):
                return columns[number * 16 : (number + 1) * 16]

            centre[col, 0:16] = group(27)
            for rate in range(3):
                for col_tap in range(3):
                    summed = group(rate * 9 + 3 + col_tap)
                    summed = summed + shifted(group(rate * 9 + col_tap), -RATES[rate])
                    summed = summed + shifted(group(rate * 9 + 6 + col_tap), RATES[rate])
                    if col_tap == 1:
                        centre[col, 16 * (rate + 1) : 16 * (rate + 2)] = summed
                    else:
                        sides[2 * rate + col_tap // 2][col] = summed.astype(BF)
            total[...] += group(28)
        return carry

    for copy in loads + copies[0]:
        copy.wait()
    lax.fori_loop(0, 3, pair, 0)
    for copy in copies[1]:
        copy.wait()
    lax.fori_loop(3, 6, pair, 0)
    strip = jnp.sum(total[...], axis=1, keepdims=True)
    high = strip.astype(BF).astype(F32)
    middle = (strip - high).astype(BF).astype(F32)
    low = strip - high - middle
    terms = jnp.where(lane == 0, high, jnp.where(lane == 1, middle, jnp.where(lane == 2, low, 0.0)))
    terms = terms.astype(BF)
    for rate in range(3):
        for way in range(2):
            sides[2 * rate + way][SIZES[rate] - 1] = terms
    opposite[4] = terms
    for edge in range(2):
        for way in range(2):
            near, middle_rate, far = sides[way], sides[2 + way], sides[4 + way]
            here, there = (edge, 10 + edge) if way == 0 else (10 + edge, edge)
            for branch in range(4):
                piece = centre[there, 16 * branch : 16 * (branch + 1)]
                near[12 + 2 * branch + edge] = piece.astype(BF)
            near[20 + edge] = middle_rate[here]
            middle_rate[12 + edge] = near[there]
            middle_rate[14 + edge] = far[here]
            far[12 + edge] = middle_rate[there]
            opposite[2 - 2 * way + edge] = far[there]


def products(pieces, atrous, point, pool):
    depth = atrous.shape[1]
    sides = [jax.ShapeDtypeStruct((size, 16, MAP_ROWS), BF) for size in SIZES for _ in range(2)]
    anywhere = pl.BlockSpec(memory_space=pl.ANY)
    return pl.pallas_call(
        products_kernel,
        out_shape=[jax.ShapeDtypeStruct((12, 64, MAP_ROWS), F32)]
        + sides
        + [jax.ShapeDtypeStruct((5, 16, MAP_ROWS), BF)],
        in_specs=[anywhere] * 19,
        scratch_shapes=[
            pltpu.VMEM((12, 16, 8, depth), BF),
            pltpu.VMEM((464, depth), BF),
            pltpu.VMEM((16, MAP_ROWS), F32),
            pltpu.SemaphoreType.DMA((2 * len(PIECES),)),
            pltpu.SemaphoreType.DMA((3,)),
        ],
        compiler_params=pltpu.CompilerParams(vmem_limit_bytes=VMEM_BYTES),
        name="products",
    )(*pieces, atrous, point, pool)


def branches_kernel(centre, *refs):
    sides = refs[0:6]
    opposite, own_left, own_right, own_terms, bias, top, bottom = refs[6:13]
    out, rows, slots = refs[13:16]
    strip = lax.axis_index("col")

    diagonal = lax.broadcasted_iota(jnp.int32, (16, 16), 0) == lax.broadcasted_iota(
        jnp.int32, (16, 16), 1
    )

    def bias_column(branch):
        row = jnp.broadcast_to(bias[branch : branch + 1], (16, 16))
        return jnp.sum(jnp.where(diagonal, row, 0.0), axis=1, keepdims=True)

    def brought(distance, index):
        ref = opposite
        if abs(distance) < 4:
            ref = sides[2 * (abs(distance) - 1) + (1 if distance > 0 else 0)]
        source = strip + distance
        inside = (source >= 0) & (source < 8)
        return jnp.where(inside, ref[index].astype(F32), 0.0)

    def column(c16):
        if 2 <= c16 < 14:
            col = c16 - 2
            values = [centre[col, 0:16]]
            for rate in range(3):
                running = centre[col, 16 * (rate + 1) : 16 * (rate + 2)]
                values.append(running + brought(-rate - 1, col) + brought(rate + 1, col))
            return values
        edge = c16 % 2
        side = -1 if c16 < 2 else 1
        own = own_right[10 + edge] if side < 0 else own_left[edge]
        values = [brought(side, 12 + 2 * branch + edge) for branch in range(4)]
        last = 2 + edge if side < 0 else edge
        values[1] = values[1] + brought(2 * side, 12 + edge) + own.astype(F32)
        values[2] = values[2] + brought(3 * side, 12 + edge) + brought(-side, 20 + edge)
        values[3] = values[3] + brought(4 * side, last) + brought(-2 * side, 14 + edge)
        return values

    for c8 in range(8):
        values = column(c8) + column(c8 + 8)
        biases = [bias_column(k % 4) for k in range(8)]
        block = jnp.concatenate([v + b for v, b in zip(values, biases)], axis=0)
        rows[c8, 0:8] = jnp.zeros((8, 128), F32)
        rows[c8, 8:136] = jnp.maximum(block, 0.0).T
        rows[c8, 136:144] = jnp.zeros((8, 128), F32)
    terms = own_terms[4].astype(F32) + opposite[4].astype(F32)
    for rate in range(3):
        for way in range(2):
            terms = terms + sides[2 * rate + way][SIZES[rate] - 1].astype(F32)
    mean = jnp.sum(terms, axis=1, keepdims=True) / (MAP_ROWS * MAP_COLS)
    branch = jnp.maximum(mean + bias_column(4), 0.0)
    wide = jnp.concatenate(
        [jnp.broadcast_to(branch, (16, 128)), jnp.zeros((112, 128), F32)], axis=0
    ).T
    row_index = lax.axis_index("row_0") * 4 + lax.axis_index("row_1")
    above, below = top[...].astype(F32), bottom[...].astype(F32)
    for slot in range(16):
        for c8 in range(8):
            slots[slot, c8 * 12 : c8 * 12 + 12] = rows[c8, 8 * slot + 6 : 8 * slot + 18]
        slots[slot, 96:104] = wide[0:8]
        slots[slot, 104:136] = jnp.where(slot == row_index + 1, below, above)
        out[slot] = slots[slot].astype(BF)


def branches(centre, moved, opposite, own_left, own_right, own_terms, bias, top, bottom):
    vmem = pl.BlockSpec(memory_space=pltpu.VMEM)
    return pl.pallas_call(
        branches_kernel,
        out_shape=jax.ShapeDtypeStruct((16, SLOT, 128), BF),
        in_specs=[vmem] * 14,
        scratch_shapes=[pltpu.VMEM((8, 144, 128), F32), pltpu.VMEM((16, SLOT, 128), F32)],
        compiler_params=pltpu.CompilerParams(vmem_limit_bytes=VMEM_BYTES),
        name="branches",
    )(centre, *moved, opposite, own_left, own_right, own_terms, bias, top, bottom)


def coarse_tile(received, weight, pool_weight, bias):
    lane = lax.broadcasted_iota(jnp.int32, (104, 128), 1)
    blocks = [received[source, 0:104].astype(F32) for source in range(16)]
    turned = [pltpu.roll(block, 64, 1) for block in blocks]
    halves = []
    for half in range(2):
        pieces = []
        for source in range(0, 16, 2):
            left = blocks[source] if half == 0 else turned[source]
            right = turned[source + 1] if half == 0 else blocks[source + 1]
            pieces.append(jnp.where(lane < 64, left, right)[0:96])
        halves.append(jnp.concatenate(pieces, axis=1))
    stacked = jnp.concatenate(halves, axis=0).astype(BF)
    low = blocks[0][96:104]
    high = blocks[8][96:104]
    for source in range(1, 8):
        low = low + pltpu.roll(blocks[source][96:104], 16 * source, 1)
        high = high + pltpu.roll(blocks[source + 8][96:104], 16 * source, 1)
    vector = jnp.concatenate([low, high], axis=1).astype(BF)
    constant = jnp.dot(vector, pool_weight, preferred_element_type=F32)[0:1]
    summed = jnp.dot(stacked, weight, preferred_element_type=F32)
    return jnp.maximum(summed + constant + bias[...], 0.0).astype(BF)


def decode_kernel(*refs):
    received, proj, bias, spread, low_own, w1_hbm, b1, w2_hbm, b2 = refs[0:9]
    out, fine, fine_cols, mid, mid_cols, w1, w2, weight, last, low, shift, sems = refs[9:]
    loads = [
        pltpu.make_async_copy(w1_hbm, w1, sems.at[0]),
        pltpu.make_async_copy(w2_hbm, w2, sems.at[1]),
    ]
    small_loads = [
        pltpu.make_async_copy(proj.at[branch], weight.at[:, branch], sems.at[2 + branch])
        for branch in range(4)
    ]
    small_loads.append(pltpu.make_async_copy(proj.at[4], last, sems.at[6]))
    for load in small_loads + loads:
        load.start()
    row_index = lax.axis_index("row_0") * 4 + lax.axis_index("row_1")
    low[...] = low_own[...]
    shift[32:40] = jnp.zeros((8, 128), F32)
    lane = lax.broadcasted_iota(jnp.int32, (32, 128), 1)
    for side in range(2):
        source = row_index - 1 + 2 * side
        inside = (source >= 0) & (source < 16)
        block = received[jnp.clip(source, 0, 15), 104:136].astype(F32)
        for row in range(2):
            values = block if row == 0 else pltpu.roll(block, 64, 1)
            shift[0:32] = jnp.where(inside & (lane < 48), values, 0.0)
            moved = pltpu.roll(shift[2:34], 96, 1)
            front = shift[0:32] + pltpu.roll(shift[1:33], 48, 1)
            front = front + jnp.where(lane >= 96, moved, 0.0)
            filled = jnp.concatenate([front, moved[:, 0:16]], axis=1)
            at = (18 * side + row) * 32
            low[at : at + 32] = filled.astype(BF)
    for load in small_loads:
        load.wait()
    coarse = coarse_tile(
        received, weight[...].reshape(1024, 256), last[...].reshape(256, 256), bias
    )
    fine[0:640] = jnp.dot(spread[...], coarse, preferred_element_type=F32)
    fine[640:656] = jnp.zeros((16, 256), F32)
    for tap in range(3):
        fine_cols[tap] = fine[tap : tap + 640].astype(BF)
    loads[0].wait()
    acc = jnp.zeros((576, 256), F32)
    for row_tap in range(3):
        rows = slice(row_tap * 32, row_tap * 32 + 576)
        for tap in range(3):
            acc = acc + jnp.dot(
                fine_cols[tap, rows], w1[row_tap, tap, 0:256], preferred_element_type=F32
            )
        small = jnp.concatenate([w1[row_tap, tap, 256:304] for tap in range(3)], axis=0)
        acc = acc + jnp.dot(low[rows], small, preferred_element_type=F32)
    at = lax.broadcasted_iota(jnp.int32, (576, 256), 0)
    y = 16 * row_index - 1 + (at >> 5)
    x = 24 * lax.axis_index("col") - 1 + (at & 31)
    inside = (y >= 0) & (y < 2 * MAP_ROWS) & (x >= 0) & (x < 2 * MAP_COLS)
    mid[0:576] = jnp.where(inside, jnp.maximum(acc + b1[...], 0.0), 0.0)
    mid[576:592] = jnp.zeros((16, 256), F32)
    for tap in range(3):
        mid_cols[tap] = mid[tap : tap + 576].astype(BF)
    loads[1].wait()
    acc = jnp.zeros((512, 256), F32)
    for row_tap in range(3):
        for tap in range(3):
            acc = acc + jnp.dot(
                mid_cols[tap, row_tap * 32 : row_tap * 32 + 512],
                w2[row_tap, tap],
                preferred_element_type=F32,
            )
    result = jnp.maximum(acc + b2[...], 0.0).astype(BF).reshape(16, 32, 256)
    out[...] = result[:, 0:24]


def decode(received, proj, bias, spread, low, w1, b1, w2, b2):
    vmem = pl.BlockSpec(memory_space=pltpu.VMEM)
    hbm = pl.BlockSpec(memory_space=pl.ANY)
    return pl.pallas_call(
        decode_kernel,
        out_shape=jax.ShapeDtypeStruct((16, 24, 256), BF),
        in_specs=[vmem, hbm, vmem, vmem, vmem, hbm, vmem, hbm, vmem],
        scratch_shapes=[
            pltpu.VMEM((656, 256), F32),
            pltpu.VMEM((3, 640, 256), BF),
            pltpu.VMEM((592, 256), F32),
            pltpu.VMEM((3, 576, 256), BF),
            pltpu.VMEM(w1.shape, BF),
            pltpu.VMEM(w2.shape, BF),
            pltpu.VMEM((16, 4, 16, 256), BF),
            pltpu.VMEM((16, 16, 256), BF),
            pltpu.VMEM((640, 144), BF),
            pltpu.VMEM((40, 128), F32),
            pltpu.SemaphoreType.DMA((7,)),
        ],
        compiler_params=pltpu.CompilerParams(vmem_limit_bytes=VMEM_BYTES),
        name="decode",
    )(received, proj, bias, spread, low, w1, b1, w2, b2)


def spread_kernel(out):
    n = lax.broadcasted_iota(jnp.int32, (640, 192), 0)
    m = lax.broadcasted_iota(jnp.int32, (640, 192), 1)
    col = (m * 683) >> 13
    row_index = lax.axis_index("row_0") * 4 + lax.axis_index("row_1")
    strip = lax.axis_index("col")

    def weights(fine, size, coarse):
        near = fine >> 1
        other = jnp.where((fine & 1) == 1, near + 1, near - 1)
        other = jnp.clip(other, 0, size - 1)
        value = jnp.where(coarse == near, 0.75, 0.0) + jnp.where(coarse == other, 0.25, 0.0)
        return jnp.where((fine >= 0) & (fine < 2 * size), value, 0.0)

    rows = weights(16 * row_index - 2 + (n >> 5), MAP_ROWS, 8 * row_index - 2 + m - 12 * col)
    cols = weights(24 * strip - 2 + (n & 31), MAP_COLS, 12 * strip - 2 + col)
    out[...] = (rows * cols).astype(BF)


def spread_matrix():
    return pl.pallas_call(
        spread_kernel,
        out_shape=jax.ShapeDtypeStruct((640, 192), BF),
        name="spread",
    )()


def reduce_low(low_level, weight, bias):
    reduced = jnp.dot(
        low_level.reshape(-1, low_level.shape[2]), weight, preferred_element_type=F32
    )
    reduced = jnp.maximum(reduced + bias, 0.0).astype(BF).reshape(16, 24, -1)
    return reduced


def low_columns(wide):
    full = jnp.pad(wide, ((2, 3), (0, 4), (0, 0))).reshape(672, -1)
    return jnp.concatenate([full[tap : tap + 640] for tap in range(3)], axis=1)


def border(rows):
    padded = jnp.pad(rows, ((0, 0), (0, 4), (0, 16)))
    return jnp.concatenate([padded[0], padded[1]], axis=1)


def on_device(
    features,
    low_level,
    point_weight,
    atrous_weight,
    pool_weight,
    aspp_bias,
    proj_weight,
    proj_bias,
    low_weight,
    low_bias,
    conv1_weight,
    conv1_bias,
    conv2_weight,
    conv2_bias,
):
    in_width = features.shape[2]
    tile = jnp.transpose(features, (1, 0, 2))
    reduced = reduce_low(low_level, low_weight, low_bias)
    before = next_to(reduced[:, 22:24], "col", 1)
    after = next_to(reduced[:, 0:2], "col", -1)
    wide = jnp.concatenate([before, reduced, after], axis=1)
    low, top, bottom = low_columns(wide), border(wide[0:2]), border(wide[14:16])
    pieces = gather_strip(tile[:6], "row_1", "row_0")
    pieces += gather_strip(tile[6:], "row_0", "row_1")
    spread = spread_matrix()
    atrous = jnp.transpose(atrous_weight, (0, 1, 2, 4, 3)).reshape(432, in_width)
    centre, *sides, opposite = products(pieces, atrous, point_weight.T, pool_weight.T)
    moved = []
    for rate in range(3):
        moved.append(around(sides[2 * rate], "col", rate + 1))
        moved.append(around(sides[2 * rate + 1], "col", -rate - 1))
    across = around(opposite, "col", 4)
    mine = branches(
        centre, moved, across, sides[0], sides[1], opposite, aspp_bias, top, bottom
    )
    received = lax.all_to_all(mine, ROW, split_axis=0, concat_axis=0, tiled=True)
    return decode(
        received,
        proj_weight.reshape(5, 16, 16, 256),
        proj_bias.reshape(1, 256),
        spread,
        low,
        conv1_weight,
        conv1_bias.reshape(1, 256),
        conv2_weight,
        conv2_bias.reshape(1, 256),
    )


def solution(mesh):
    torus = Mesh(
        mesh.devices.reshape(mesh.shape["dp"], 4, 4, mesh.shape["col"]),
        ("dp", "row_0", "row_1", "col"),
    )
    placed = (
        P(DP_ROW, "col", None),
        P(DP_ROW, "col", None),
        P(None, ROW),
        P(None, None, None, None, ROW),
        P(None, ROW),
        P(None, ROW),
        P(),
        P(),
        P(),
        P(),
        P(),
        P(),
        P(),
        P(),
    )
    return jax.shard_map(
        on_device, mesh=torus, in_specs=placed, out_specs=P(DP_ROW, "col", None), check_vma=False
    )
```

```python
import jax
import jax.numpy as jnp
from jax import lax
from jax.experimental import pallas as pl
from jax.experimental.pallas import tpu as pltpu
from jax.sharding import Mesh
from jax.sharding import PartitionSpec as P

ROW = ("row_0", "row_1")
DP_ROW = ("dp", "row_0", "row_1")
RATES = (12, 24, 36)
MAP_ROWS = 128
MAP_COLS = 96
BF = jnp.bfloat16
F32 = jnp.float32
VMEM_BYTES = 56 * 1024 * 1024


def around(value, axis, by):
    devices = lax.axis_size(axis)
    return lax.ppermute(value, axis, [(i, (i + by) % devices) for i in range(devices)])


def next_to(value, axis, by):
    devices = lax.axis_size(axis)
    pairs = [(i, i + by) for i in range(devices) if 0 <= i + by < devices]
    return lax.ppermute(value, axis, pairs)


def swap(value, axis, near):
    pairs = ((0, 1), (2, 3)) if near else ((0, 3), (1, 2))
    return lax.ppermute(value, axis, [way for a, b in pairs for way in ((a, b), (b, a))])


def on_chip(value):
    return pltpu.with_memory_space_constraint(value, pltpu.VMEM)


OWN, NEAR, WRAP, FAR = range(4)


def position(index, kind):
    if kind == OWN:
        return index
    if kind == NEAR:
        return index + 1 - 2 * (index % 2)
    if kind == WRAP:
        return 3 - index
    return (index + 2) % 4


def gather_strip(half, first, second):
    near = swap(half, first, True)
    wrap = swap(half, first, False)
    far_low = swap(near[:3], first, False)
    far_high = swap(wrap[3:], first, True)
    low = jnp.concatenate([half, near], axis=0)
    high = jnp.concatenate([wrap, far_low, far_high], axis=0)
    low_near = swap(low, second, True)
    low_wrap = swap(low, second, False)
    high_wrap = swap(high, second, False)
    high_near = swap(high, second, True)
    low_far = swap(low_near, second, False)
    high_far = swap(high_wrap, second, True)
    return [low, high, low_near, high_near, low_wrap, high_wrap, low_far, high_far]


LOW = ((0, 6, 0, OWN), (6, 6, 0, NEAR))
HIGH = ((0, 6, 0, WRAP), (6, 3, 0, FAR), (9, 3, 3, FAR))
PIECES = [
    (2 * which + part, *piece, kind)
    for which, kind in enumerate((OWN, NEAR, WRAP, FAR))
    for part, pieces in enumerate((LOW, HIGH))
    for piece in pieces
]
SIZES = (23, 17, 15)
SLOT = 136


def products_kernel(*refs):
    refs = (None, *refs)
    parts = (refs[1:9], refs[9:17])
    atrous, point, pool = refs[17:20]
    centre = refs[20]
    sides = refs[21:27]
    opposite = refs[27]
    feats, weights, total, feat_sems, weight_sems = refs[28:33]
    own_y, own_x = lax.axis_index("row_0"), lax.axis_index("row_1")
    copies = []
    for colour in range(2):
        group = []
        for number, (which, start, count, col, first, second) in enumerate(PIECES):
            kind_y, kind_x = (second, first) if colour == 0 else (first, second)
            tile = position(own_y, kind_y) * 4 + position(own_x, kind_x)
            group.append(
                pltpu.make_async_copy(
                    parts[colour][which].at[pl.ds(start, count)],
                    feats.at[pl.ds(6 * colour + col, count), tile],
                    feat_sems.at[colour * len(PIECES) + number],
                )
            )
        copies.append(group)
    loads = [
        pltpu.make_async_copy(atrous, weights.at[pl.ds(0, 432)], weight_sems.at[0]),
        pltpu.make_async_copy(point, weights.at[pl.ds(432, 16)], weight_sems.at[1]),
        pltpu.make_async_copy(pool, weights.at[pl.ds(448, 16)], weight_sems.at[2]),
    ]
    for copy in loads + copies[0] + copies[1]:
        copy.start()
    total[...] = jnp.zeros_like(total)
    lane = lax.broadcasted_iota(jnp.int32, (16, MAP_ROWS), 1)

    def shifted(value, offset):
        if offset == 0:
            return value
        moved = pltpu.roll(value, (-offset) % MAP_ROWS, 1)
        inside = (lane + offset >= 0) & (lane + offset < MAP_ROWS)
        return jnp.where(inside, moved, 0.0)

    def pair(index, carry):
        block = feats[pl.ds(2 * index, 2)].reshape(2 * MAP_ROWS, feats.shape[-1])
        result = lax.dot_general(
            weights[...], block, (((1,), (1,)), ((), ())), preferred_element_type=F32
        )
        for side in range(2):
            col = 2 * index + side
            columns = result[:, side * MAP_ROWS : (side + 1) * MAP_ROWS]

            def group(number, columns=columns):
                return columns[number * 16 : (number + 1) * 16]

            centre[col, 0:16] = group(27)
            for rate in range(3):
                for col_tap in range(3):
                    summed = group(rate * 9 + 3 + col_tap)
                    summed = summed + shifted(group(rate * 9 + col_tap), -RATES[rate])
                    summed = summed + shifted(group(rate * 9 + 6 + col_tap), RATES[rate])
                    if col_tap == 1:
                        centre[col, 16 * (rate + 1) : 16 * (rate + 2)] = summed
                    else:
                        sides[2 * rate + col_tap // 2][col] = summed.astype(BF)
            total[...] += group(28)
        return carry

    for copy in loads + copies[0]:
        copy.wait()
    lax.fori_loop(0, 3, pair, 0)
    for copy in copies[1]:
        copy.wait()
    lax.fori_loop(3, 6, pair, 0)
    strip = jnp.sum(total[...], axis=1, keepdims=True)
    high = strip.astype(BF).astype(F32)
    middle = (strip - high).astype(BF).astype(F32)
    low = strip - high - middle
    terms = jnp.where(lane == 0, high, jnp.where(lane == 1, middle, jnp.where(lane == 2, low, 0.0)))
    terms = terms.astype(BF)
    for rate in range(3):
        for way in range(2):
            sides[2 * rate + way][SIZES[rate] - 1] = terms
    opposite[4] = terms
    for edge in range(2):
        for way in range(2):
            near, middle_rate, far = sides[way], sides[2 + way], sides[4 + way]
            here, there = (edge, 10 + edge) if way == 0 else (10 + edge, edge)
            for branch in range(4):
                piece = centre[there, 16 * branch : 16 * (branch + 1)]
                near[12 + 2 * branch + edge] = piece.astype(BF)
            near[20 + edge] = middle_rate[here]
            middle_rate[12 + edge] = near[there]
            middle_rate[14 + edge] = far[here]
            far[12 + edge] = middle_rate[there]
            opposite[2 - 2 * way + edge] = far[there]


def products(pieces, atrous, point, pool):
    depth = atrous.shape[1]
    sides = [pltpu.VMEM((size, 16, MAP_ROWS), BF) for size in SIZES for _ in range(2)]
    anywhere = pl.BlockSpec(memory_space=pl.ANY)
    return pl.pallas_call(
        products_kernel,
        out_shape=[pltpu.VMEM((12, 64, MAP_ROWS), F32)]
        + sides
        + [pltpu.VMEM((5, 16, MAP_ROWS), BF)],
        in_specs=[anywhere] * 19,
        scratch_shapes=[
            pltpu.VMEM((12, 16, 8, depth), BF),
            pltpu.VMEM((464, depth), BF),
            pltpu.VMEM((16, MAP_ROWS), F32),
            pltpu.SemaphoreType.DMA((2 * len(PIECES),)),
            pltpu.SemaphoreType.DMA((3,)),
        ],
        compiler_params=pltpu.CompilerParams(vmem_limit_bytes=VMEM_BYTES),
        name="products",
    )(*pieces, atrous, point, pool)


def branches_kernel(centre, *refs):
    sides = refs[0:6]
    opposite, own_left, own_right, own_terms, bias, top, bottom = refs[6:13]
    out, rows, slots = refs[13:16]
    strip = lax.axis_index("col")

    diagonal = lax.broadcasted_iota(jnp.int32, (16, 16), 0) == lax.broadcasted_iota(
        jnp.int32, (16, 16), 1
    )

    def bias_column(branch):
        row = jnp.broadcast_to(bias[branch : branch + 1], (16, 16))
        return jnp.sum(jnp.where(diagonal, row, 0.0), axis=1, keepdims=True)

    def brought(distance, index):
        ref = opposite
        if abs(distance) < 4:
            ref = sides[2 * (abs(distance) - 1) + (1 if distance > 0 else 0)]
        source = strip + distance
        inside = (source >= 0) & (source < 8)
        return jnp.where(inside, ref[index].astype(F32), 0.0)

    def column(c16):
        if 2 <= c16 < 14:
            col = c16 - 2
            values = [centre[col, 0:16]]
            for rate in range(3):
                running = centre[col, 16 * (rate + 1) : 16 * (rate + 2)]
                values.append(running + brought(-rate - 1, col) + brought(rate + 1, col))
            return values
        edge = c16 % 2
        side = -1 if c16 < 2 else 1
        own = own_right[10 + edge] if side < 0 else own_left[edge]
        values = [brought(side, 12 + 2 * branch + edge) for branch in range(4)]
        last = 2 + edge if side < 0 else edge
        values[1] = values[1] + brought(2 * side, 12 + edge) + own.astype(F32)
        values[2] = values[2] + brought(3 * side, 12 + edge) + brought(-side, 20 + edge)
        values[3] = values[3] + brought(4 * side, last) + brought(-2 * side, 14 + edge)
        return values

    for c8 in range(8):
        values = column(c8) + column(c8 + 8)
        biases = [bias_column(k % 4) for k in range(8)]
        block = jnp.concatenate([v + b for v, b in zip(values, biases)], axis=0)
        rows[c8, 0:8] = jnp.zeros((8, 128), F32)
        rows[c8, 8:136] = jnp.maximum(block, 0.0).T
        rows[c8, 136:144] = jnp.zeros((8, 128), F32)
    terms = own_terms[4].astype(F32) + opposite[4].astype(F32)
    for rate in range(3):
        for way in range(2):
            terms = terms + sides[2 * rate + way][SIZES[rate] - 1].astype(F32)
    mean = jnp.sum(terms, axis=1, keepdims=True) / (MAP_ROWS * MAP_COLS)
    branch = jnp.maximum(mean + bias_column(4), 0.0)
    wide = jnp.concatenate(
        [jnp.broadcast_to(branch, (16, 128)), jnp.zeros((112, 128), F32)], axis=0
    ).T
    row_index = lax.axis_index("row_0") * 4 + lax.axis_index("row_1")
    above, below = top[...].astype(F32), bottom[...].astype(F32)
    for slot in range(16):
        for c8 in range(8):
            slots[slot, c8 * 12 : c8 * 12 + 12] = rows[c8, 8 * slot + 6 : 8 * slot + 18]
        slots[slot, 96:104] = wide[0:8]
        slots[slot, 104:136] = jnp.where(slot == row_index + 1, below, above)
        out[slot] = slots[slot].astype(BF)


def branches(centre, moved, opposite, own_left, own_right, own_terms, bias, top, bottom):
    vmem = pl.BlockSpec(memory_space=pltpu.VMEM)
    return pl.pallas_call(
        branches_kernel,
        out_shape=pltpu.VMEM((16, SLOT, 128), BF),
        in_specs=[vmem] * 14,
        scratch_shapes=[pltpu.VMEM((8, 144, 128), F32), pltpu.VMEM((16, SLOT, 128), F32)],
        compiler_params=pltpu.CompilerParams(vmem_limit_bytes=VMEM_BYTES),
        name="branches",
    )(*map(on_chip, (centre, *moved, opposite, own_left, own_right, own_terms)), bias, top, bottom)


def coarse_tile(received, weight, pool_weight, bias):
    lane = lax.broadcasted_iota(jnp.int32, (104, 128), 1)
    blocks = [received[source, 0:104].astype(F32) for source in range(16)]
    turned = [pltpu.roll(block, 64, 1) for block in blocks]
    halves = []
    for half in range(2):
        pieces = []
        for source in range(0, 16, 2):
            left = blocks[source] if half == 0 else turned[source]
            right = turned[source + 1] if half == 0 else blocks[source + 1]
            pieces.append(jnp.where(lane < 64, left, right)[0:96])
        halves.append(jnp.concatenate(pieces, axis=1))
    stacked = jnp.concatenate(halves, axis=0).astype(BF)
    low = blocks[0][96:104]
    high = blocks[8][96:104]
    for source in range(1, 8):
        low = low + pltpu.roll(blocks[source][96:104], 16 * source, 1)
        high = high + pltpu.roll(blocks[source + 8][96:104], 16 * source, 1)
    vector = jnp.concatenate([low, high], axis=1).astype(BF)
    constant = jnp.dot(vector, pool_weight, preferred_element_type=F32)[0:1]
    summed = jnp.dot(stacked, weight, preferred_element_type=F32)
    return jnp.maximum(summed + constant + bias[...], 0.0).astype(BF)


def decode_kernel(*refs):
    received, proj, bias, spread, low_own, w1_hbm, b1, w2_hbm, b2 = refs[0:9]
    out, fine, fine_cols, mid, mid_cols, w1, w2, weight, last, low, shift, sems = refs[9:]
    loads = [
        pltpu.make_async_copy(w1_hbm, w1, sems.at[0]),
        pltpu.make_async_copy(w2_hbm, w2, sems.at[1]),
    ]
    small_loads = [
        pltpu.make_async_copy(proj.at[branch], weight.at[:, branch], sems.at[2 + branch])
        for branch in range(4)
    ]
    small_loads.append(pltpu.make_async_copy(proj.at[4], last, sems.at[6]))
    for load in small_loads + loads:
        load.start()
    row_index = lax.axis_index("row_0") * 4 + lax.axis_index("row_1")
    low[...] = low_own[...]
    shift[32:40] = jnp.zeros((8, 128), F32)
    lane = lax.broadcasted_iota(jnp.int32, (32, 128), 1)
    for side in range(2):
        source = row_index - 1 + 2 * side
        inside = (source >= 0) & (source < 16)
        block = received[jnp.clip(source, 0, 15), 104:136].astype(F32)
        for row in range(2):
            values = block if row == 0 else pltpu.roll(block, 64, 1)
            shift[0:32] = jnp.where(inside & (lane < 48), values, 0.0)
            moved = pltpu.roll(shift[2:34], 96, 1)
            front = shift[0:32] + pltpu.roll(shift[1:33], 48, 1)
            front = front + jnp.where(lane >= 96, moved, 0.0)
            filled = jnp.concatenate([front, moved[:, 0:16]], axis=1)
            at = (18 * side + row) * 32
            low[at : at + 32] = filled.astype(BF)
    for load in small_loads:
        load.wait()
    coarse = coarse_tile(
        received, weight[...].reshape(1024, 256), last[...].reshape(256, 256), bias
    )
    fine[0:640] = jnp.dot(spread[...], coarse, preferred_element_type=F32)
    fine[640:656] = jnp.zeros((16, 256), F32)
    for tap in range(3):
        fine_cols[tap] = fine[tap : tap + 640].astype(BF)
    loads[0].wait()
    acc = jnp.zeros((576, 256), F32)
    for row_tap in range(3):
        rows = slice(row_tap * 32, row_tap * 32 + 576)
        for tap in range(3):
            acc = acc + jnp.dot(
                fine_cols[tap, rows], w1[row_tap, tap, 0:256], preferred_element_type=F32
            )
        small = jnp.concatenate([w1[row_tap, tap, 256:304] for tap in range(3)], axis=0)
        acc = acc + jnp.dot(low[rows], small, preferred_element_type=F32)
    at = lax.broadcasted_iota(jnp.int32, (576, 256), 0)
    y = 16 * row_index - 1 + (at >> 5)
    x = 24 * lax.axis_index("col") - 1 + (at & 31)
    inside = (y >= 0) & (y < 2 * MAP_ROWS) & (x >= 0) & (x < 2 * MAP_COLS)
    mid[0:576] = jnp.where(inside, jnp.maximum(acc + b1[...], 0.0), 0.0)
    mid[576:592] = jnp.zeros((16, 256), F32)
    for tap in range(3):
        mid_cols[tap] = mid[tap : tap + 576].astype(BF)
    loads[1].wait()
    acc = jnp.zeros((512, 256), F32)
    for row_tap in range(3):
        for tap in range(3):
            acc = acc + jnp.dot(
                mid_cols[tap, row_tap * 32 : row_tap * 32 + 512],
                w2[row_tap, tap],
                preferred_element_type=F32,
            )
    result = jnp.maximum(acc + b2[...], 0.0).astype(BF).reshape(16, 32, 256)
    out[...] = result[:, 0:24]


def decode(received, proj, bias, spread, low, w1, b1, w2, b2):
    vmem = pl.BlockSpec(memory_space=pltpu.VMEM)
    hbm = pl.BlockSpec(memory_space=pl.ANY)
    return pl.pallas_call(
        decode_kernel,
        out_shape=jax.ShapeDtypeStruct((16, 24, 256), BF),
        in_specs=[vmem, hbm, vmem, vmem, vmem, hbm, vmem, hbm, vmem],
        scratch_shapes=[
            pltpu.VMEM((656, 256), F32),
            pltpu.VMEM((3, 640, 256), BF),
            pltpu.VMEM((592, 256), F32),
            pltpu.VMEM((3, 576, 256), BF),
            pltpu.VMEM(w1.shape, BF),
            pltpu.VMEM(w2.shape, BF),
            pltpu.VMEM((16, 4, 16, 256), BF),
            pltpu.VMEM((16, 16, 256), BF),
            pltpu.VMEM((640, 144), BF),
            pltpu.VMEM((40, 128), F32),
            pltpu.SemaphoreType.DMA((7,)),
        ],
        compiler_params=pltpu.CompilerParams(vmem_limit_bytes=VMEM_BYTES),
        name="decode",
    )(on_chip(received), proj, bias, on_chip(spread), on_chip(low), w1, b1, w2, b2)


def spread_kernel(out):
    n = lax.broadcasted_iota(jnp.int32, (640, 192), 0)
    m = lax.broadcasted_iota(jnp.int32, (640, 192), 1)
    col = (m * 683) >> 13
    row_index = lax.axis_index("row_0") * 4 + lax.axis_index("row_1")
    strip = lax.axis_index("col")

    def weights(fine, size, coarse):
        near = fine >> 1
        other = jnp.where((fine & 1) == 1, near + 1, near - 1)
        other = jnp.clip(other, 0, size - 1)
        value = jnp.where(coarse == near, 0.75, 0.0) + jnp.where(coarse == other, 0.25, 0.0)
        return jnp.where((fine >= 0) & (fine < 2 * size), value, 0.0)

    rows = weights(16 * row_index - 2 + (n >> 5), MAP_ROWS, 8 * row_index - 2 + m - 12 * col)
    cols = weights(24 * strip - 2 + (n & 31), MAP_COLS, 12 * strip - 2 + col)
    out[...] = (rows * cols).astype(BF)


def spread_matrix():
    return pl.pallas_call(
        spread_kernel,
        out_shape=pltpu.VMEM((640, 192), BF),
        name="spread",
    )()


def reduce_low(low_level, weight, bias):
    reduced = jnp.dot(
        low_level.reshape(-1, low_level.shape[2]), weight, preferred_element_type=F32
    )
    reduced = jnp.maximum(reduced + bias, 0.0).astype(BF).reshape(16, 24, -1)
    return reduced


def low_columns(wide):
    full = jnp.pad(wide, ((2, 3), (0, 4), (0, 0))).reshape(672, -1)
    return jnp.concatenate([full[tap : tap + 640] for tap in range(3)], axis=1)


def border(rows):
    padded = jnp.pad(rows, ((0, 0), (0, 4), (0, 16)))
    return jnp.concatenate([padded[0], padded[1]], axis=1)


def on_device(
    features,
    low_level,
    point_weight,
    atrous_weight,
    pool_weight,
    aspp_bias,
    proj_weight,
    proj_bias,
    low_weight,
    low_bias,
    conv1_weight,
    conv1_bias,
    conv2_weight,
    conv2_bias,
):
    in_width = features.shape[2]
    tile = jnp.transpose(features, (1, 0, 2))
    reduced = reduce_low(low_level, low_weight, low_bias)
    before = next_to(reduced[:, 22:24], "col", 1)
    after = next_to(reduced[:, 0:2], "col", -1)
    wide = jnp.concatenate([before, reduced, after], axis=1)
    low, top, bottom = low_columns(wide), border(wide[0:2]), border(wide[14:16])
    pieces = gather_strip(tile[:6], "row_1", "row_0")
    pieces += gather_strip(tile[6:], "row_0", "row_1")
    spread = spread_matrix()
    atrous = jnp.transpose(atrous_weight, (0, 1, 2, 4, 3)).reshape(432, in_width)
    centre, *sides, opposite = products(pieces, atrous, point_weight.T, pool_weight.T)
    moved = []
    for rate in range(3):
        moved.append(around(sides[2 * rate], "col", rate + 1))
        moved.append(around(sides[2 * rate + 1], "col", -rate - 1))
    across = around(opposite, "col", 4)
    mine = branches(
        centre, moved, across, sides[0], sides[1], opposite, aspp_bias, top, bottom
    )
    received = lax.all_to_all(mine, ROW, split_axis=0, concat_axis=0, tiled=True)
    return decode(
        received,
        proj_weight.reshape(5, 16, 16, 256),
        proj_bias.reshape(1, 256),
        spread,
        low,
        conv1_weight,
        conv1_bias.reshape(1, 256),
        conv2_weight,
        conv2_bias.reshape(1, 256),
    )


def solution(mesh):
    torus = Mesh(
        mesh.devices.reshape(mesh.shape["dp"], 4, 4, mesh.shape["col"]),
        ("dp", "row_0", "row_1", "col"),
    )
    placed = (
        P(DP_ROW, "col", None),
        P(DP_ROW, "col", None),
        P(None, ROW),
        P(None, None, None, None, ROW),
        P(None, ROW),
        P(None, ROW),
        P(),
        P(),
        P(),
        P(),
        P(),
        P(),
        P(),
        P(),
    )
    return jax.shard_map(
        on_device, mesh=torus, in_specs=placed, out_specs=P(DP_ROW, "col", None), check_vma=False
    )
```

```python
import functools

import jax
import jax.numpy as jnp
from jax import lax
from jax.experimental import pallas as pl
from jax.experimental.pallas import tpu as pltpu
from jax.sharding import Mesh
from jax.sharding import PartitionSpec as P

ROW = ("row_0", "row_1")
DP_ROW = ("dp", "row_0", "row_1")
RATES = (12, 24, 36)
MAP_ROWS = 128
MAP_COLS = 96
BF = jnp.bfloat16
F32 = jnp.float32
VMEM_BYTES = 32 * 1024 * 1024


def around(value, axis, by):
    devices = lax.axis_size(axis)
    return lax.ppermute(value, axis, [(i, (i + by) % devices) for i in range(devices)])


def next_to(value, axis, by):
    devices = lax.axis_size(axis)
    pairs = [(i, i + by) for i in range(devices) if 0 <= i + by < devices]
    return lax.ppermute(value, axis, pairs)


def swap(value, axis, near):
    pairs = ((0, 1), (2, 3)) if near else ((0, 3), (1, 2))
    return lax.ppermute(value, axis, [way for a, b in pairs for way in ((a, b), (b, a))])


def on_chip(value):
    return pltpu.with_memory_space_constraint(value, pltpu.VMEM)


OWN, NEAR, WRAP, FAR = range(4)


def position(index, kind):
    if kind == OWN:
        return index
    if kind == NEAR:
        return index + 1 - 2 * (index % 2)
    if kind == WRAP:
        return 3 - index
    return (index + 2) % 4


def gather_strip(half, first, second):
    near = swap(half, first, True)
    wrap = swap(half, first, False)
    far_low = swap(near[:3], first, False)
    far_high = swap(wrap[3:], first, True)
    low = jnp.concatenate([half, near], axis=0)
    high = jnp.concatenate([wrap, far_low, far_high], axis=0)
    low_near = swap(low, second, True)
    low_wrap = swap(low, second, False)
    high_wrap = swap(high, second, False)
    high_near = swap(high, second, True)
    low_far = swap(low_near, second, False)
    high_far = swap(high_wrap, second, True)
    return [low, high, low_near, high_near, low_wrap, high_wrap, low_far, high_far]


LOW = ((0, 6, 0, OWN), (6, 6, 0, NEAR))
HIGH = ((0, 6, 0, WRAP), (6, 3, 0, FAR), (9, 3, 3, FAR))
EARLY = [
    (2 * which + part, *piece, kind)
    for which, kind in enumerate((OWN, NEAR, WRAP))
    for part, pieces in enumerate((LOW, HIGH))
    for piece in pieces
]
SIZES = (23, 17, 15)
SLOT = 136


def weight_copies(atrous, point, pool, weights, sems):
    return [
        pltpu.make_async_copy(atrous, weights.at[pl.ds(0, 432)], sems.at[0]),
        pltpu.make_async_copy(point, weights.at[pl.ds(432, 16)], sems.at[1]),
        pltpu.make_async_copy(pool, weights.at[pl.ds(448, 16)], sems.at[2]),
    ]


def transposed_dot(weights, block):
    return lax.dot_general(
        weights, block, (((1,), (1,)), ((), ())), preferred_element_type=F32
    )


def early_kernel(*refs):
    parts = (refs[0:6], refs[6:12])
    atrous, point, pool, out, feats, weights, feat_sems, weight_sems = refs[12:20]
    own_y, own_x = lax.axis_index("row_0"), lax.axis_index("row_1")
    copies = []
    for colour in range(2):
        group = []
        for number, (which, start, count, col, first, second) in enumerate(EARLY):
            kind_y, kind_x = (second, first) if colour == 0 else (first, second)
            tile = position(own_y, kind_y) * 4 + position(own_x, kind_x)
            group.append(
                pltpu.make_async_copy(
                    parts[colour][which].at[pl.ds(start, count)],
                    feats.at[pl.ds(6 * colour + col, count), tile],
                    feat_sems.at[colour * len(EARLY) + number],
                )
            )
        copies.append(group)
    loads = weight_copies(atrous, point, pool, weights, weight_sems)
    for copy in loads + copies[0] + copies[1]:
        copy.start()
    zeros = jnp.zeros((6, 8, feats.shape[-1]), BF)
    for other in range(4):
        feats[0:6, position(own_y, FAR) * 4 + other] = zeros
        feats[6:12, other * 4 + position(own_x, FAR)] = zeros

    def pair(index, carry):
        block = feats[pl.ds(2 * index, 2)].reshape(2 * MAP_ROWS, feats.shape[-1])
        out[index] = transposed_dot(weights[...], block)
        return carry

    for copy in loads + copies[0]:
        copy.wait()
    lax.fori_loop(0, 3, pair, 0)
    for copy in copies[1]:
        copy.wait()
    lax.fori_loop(3, 6, pair, 0)


def early_products(pieces, atrous, point, pool):
    depth = atrous.shape[1]
    anywhere = pl.BlockSpec(memory_space=pl.ANY)
    return pl.pallas_call(
        early_kernel,
        out_shape=pltpu.VMEM((6, 464, 256), F32),
        in_specs=[anywhere] * 15,
        scratch_shapes=[
            pltpu.VMEM((12, 16, 8, depth), BF),
            pltpu.VMEM((464, depth), BF),
            pltpu.SemaphoreType.DMA((2 * len(EARLY),)),
            pltpu.SemaphoreType.DMA((3,)),
        ],
        compiler_params=pltpu.CompilerParams(vmem_limit_bytes=VMEM_BYTES),
        name="early",
    )(*pieces, atrous, point, pool)


def products_kernel(*refs):
    early, low_a, high_a, low_b, high_b, atrous, point, pool = refs[0:8]
    centre = refs[8]
    sides = refs[9:15]
    opposite = refs[15]
    feats, weights, total, far, feat_sems, weight_sems = refs[16:22]
    own_y, own_x = lax.axis_index("row_0"), lax.axis_index("row_1")
    far_y, far_x = position(own_y, FAR), position(own_x, FAR)
    copies = []
    for colour, (own, received) in enumerate(((own_x, (low_a, high_a)), (own_y, (low_b, high_b)))):
        for part, pieces in enumerate((LOW, HIGH)):
            for start, count, col, kind in pieces:
                copies.append(
                    pltpu.make_async_copy(
                        received[part].at[pl.ds(start, count)],
                        feats.at[colour, pl.ds(col, count), position(own, kind)],
                        feat_sems.at[len(copies)],
                    )
                )
    copies += weight_copies(atrous, point, pool, weights, weight_sems)
    for copy in copies:
        copy.start()
    total[...] = jnp.zeros_like(total)
    lane = lax.broadcasted_iota(jnp.int32, (16, MAP_ROWS), 1)

    def shifted(value, offset):
        if offset == 0:
            return value
        moved = pltpu.roll(value, (-offset) % MAP_ROWS, 1)
        inside = (lane + offset >= 0) & (lane + offset < MAP_ROWS)
        return jnp.where(inside, moved, 0.0)

    at = lax.broadcasted_iota(jnp.int32, (464, MAP_ROWS), 1)

    def merged(colour, inner, columns):
        chunk = far[colour, :, pl.ds(pl.multiple_of(128 * (inner // 4), 128), 128)]
        if colour == 0:
            moved = pltpu.roll(chunk, (32 * far_y - 32 * inner + 256) % 128, 1)
            return jnp.where((at >> 5) == far_y, moved, columns)
        for band in range(4):
            moved = pltpu.roll(chunk, (24 * band + 8 * far_x - 32 * inner + 256) % 128, 1)
            columns = jnp.where((at >> 3) == 4 * band + far_x, moved, columns)
        return columns

    def pair(index, carry, colour):
        for side in range(2):
            col = 2 * index + side
            columns = early[index, :, side * MAP_ROWS : (side + 1) * MAP_ROWS]
            columns = merged(colour, col - 6 * colour, columns)

            def group(number, columns=columns):
                return columns[number * 16 : (number + 1) * 16]

            centre[col, 0:16] = group(27)
            for rate in range(3):
                for col_tap in range(3):
                    summed = group(rate * 9 + 3 + col_tap)
                    summed = summed + shifted(group(rate * 9 + col_tap), -RATES[rate])
                    summed = summed + shifted(group(rate * 9 + 6 + col_tap), RATES[rate])
                    if col_tap == 1:
                        centre[col, 16 * (rate + 1) : 16 * (rate + 2)] = summed
                    else:
                        sides[2 * rate + col_tap // 2][col] = summed.astype(BF)
            total[...] += group(28)
        return carry

    for copy in copies:
        copy.wait()
    for colour in range(2):
        block = feats[colour].reshape(192, feats.shape[-1])
        far[colour, :, 0:192] = transposed_dot(weights[...], block)
    for colour in range(2):
        lax.fori_loop(3 * colour, 3 * colour + 3, functools.partial(pair, colour=colour), 0)
    strip = jnp.sum(total[...], axis=1, keepdims=True)
    high = strip.astype(BF).astype(F32)
    middle = (strip - high).astype(BF).astype(F32)
    low = strip - high - middle
    terms = jnp.where(lane == 0, high, jnp.where(lane == 1, middle, jnp.where(lane == 2, low, 0.0)))
    terms = terms.astype(BF)
    for rate in range(3):
        for way in range(2):
            sides[2 * rate + way][SIZES[rate] - 1] = terms
    opposite[4] = terms
    for edge in range(2):
        for way in range(2):
            near, middle_rate, far = sides[way], sides[2 + way], sides[4 + way]
            here, there = (edge, 10 + edge) if way == 0 else (10 + edge, edge)
            for branch in range(4):
                piece = centre[there, 16 * branch : 16 * (branch + 1)]
                near[12 + 2 * branch + edge] = piece.astype(BF)
            near[20 + edge] = middle_rate[here]
            middle_rate[12 + edge] = near[there]
            middle_rate[14 + edge] = far[here]
            far[12 + edge] = middle_rate[there]
            opposite[2 - 2 * way + edge] = far[there]


def products(early, pieces, atrous, point, pool):
    depth = atrous.shape[1]
    sides = [pltpu.VMEM((size, 16, MAP_ROWS), BF) for size in SIZES for _ in range(2)]
    anywhere = pl.BlockSpec(memory_space=pl.ANY)
    return pl.pallas_call(
        products_kernel,
        out_shape=[pltpu.VMEM((12, 64, MAP_ROWS), F32)]
        + sides
        + [pltpu.VMEM((5, 16, MAP_ROWS), BF)],
        in_specs=[pl.BlockSpec(memory_space=pltpu.VMEM)] + [anywhere] * 7,
        scratch_shapes=[
            pltpu.VMEM((2, 6, 4, 8, depth), BF),
            pltpu.VMEM((464, depth), BF),
            pltpu.VMEM((16, MAP_ROWS), F32),
            pltpu.VMEM((2, 464, 256), F32),
            pltpu.SemaphoreType.DMA((2 * (len(LOW) + len(HIGH)),)),
            pltpu.SemaphoreType.DMA((3,)),
        ],
        compiler_params=pltpu.CompilerParams(vmem_limit_bytes=VMEM_BYTES),
        name="products",
    )(on_chip(early), *pieces, atrous, point, pool)


def branches_kernel(centre, *refs):
    sides = refs[0:6]
    opposite, own_left, own_right, own_terms, bias, top, bottom = refs[6:13]
    out, rows, slots = refs[13:16]
    strip = lax.axis_index("col")

    diagonal = lax.broadcasted_iota(jnp.int32, (16, 16), 0) == lax.broadcasted_iota(
        jnp.int32, (16, 16), 1
    )

    def bias_column(branch):
        row = jnp.broadcast_to(bias[branch : branch + 1], (16, 16))
        return jnp.sum(jnp.where(diagonal, row, 0.0), axis=1, keepdims=True)

    def brought(distance, index):
        ref = opposite
        if abs(distance) < 4:
            ref = sides[2 * (abs(distance) - 1) + (1 if distance > 0 else 0)]
        source = strip + distance
        inside = (source >= 0) & (source < 8)
        return jnp.where(inside, ref[index].astype(F32), 0.0)

    def column(c16):
        if 2 <= c16 < 14:
            col = c16 - 2
            values = [centre[col, 0:16]]
            for rate in range(3):
                running = centre[col, 16 * (rate + 1) : 16 * (rate + 2)]
                values.append(running + brought(-rate - 1, col) + brought(rate + 1, col))
            return values
        edge = c16 % 2
        side = -1 if c16 < 2 else 1
        own = own_right[10 + edge] if side < 0 else own_left[edge]
        values = [brought(side, 12 + 2 * branch + edge) for branch in range(4)]
        last = 2 + edge if side < 0 else edge
        values[1] = values[1] + brought(2 * side, 12 + edge) + own.astype(F32)
        values[2] = values[2] + brought(3 * side, 12 + edge) + brought(-side, 20 + edge)
        values[3] = values[3] + brought(4 * side, last) + brought(-2 * side, 14 + edge)
        return values

    for c8 in range(8):
        values = column(c8) + column(c8 + 8)
        biases = [bias_column(k % 4) for k in range(8)]
        block = jnp.concatenate([v + b for v, b in zip(values, biases)], axis=0)
        rows[c8, 0:8] = jnp.zeros((8, 128), F32)
        rows[c8, 8:136] = jnp.maximum(block, 0.0).T
        rows[c8, 136:144] = jnp.zeros((8, 128), F32)
    terms = own_terms[4].astype(F32) + opposite[4].astype(F32)
    for rate in range(3):
        for way in range(2):
            terms = terms + sides[2 * rate + way][SIZES[rate] - 1].astype(F32)
    mean = jnp.sum(terms, axis=1, keepdims=True) / (MAP_ROWS * MAP_COLS)
    branch = jnp.maximum(mean + bias_column(4), 0.0)
    wide = jnp.concatenate(
        [jnp.broadcast_to(branch, (16, 128)), jnp.zeros((112, 128), F32)], axis=0
    ).T
    row_index = lax.axis_index("row_0") * 4 + lax.axis_index("row_1")
    above, below = top[...].astype(F32), bottom[...].astype(F32)
    for slot in range(16):
        for c8 in range(8):
            slots[slot, c8 * 12 : c8 * 12 + 12] = rows[c8, 8 * slot + 6 : 8 * slot + 18]
        slots[slot, 96:104] = wide[0:8]
        slots[slot, 104:136] = jnp.where(slot == row_index + 1, below, above)
        out[slot] = slots[slot].astype(BF)


def branches(centre, moved, opposite, own_left, own_right, own_terms, bias, top, bottom):
    vmem = pl.BlockSpec(memory_space=pltpu.VMEM)
    return pl.pallas_call(
        branches_kernel,
        out_shape=pltpu.VMEM((16, SLOT, 128), BF),
        in_specs=[vmem] * 14,
        scratch_shapes=[pltpu.VMEM((8, 144, 128), F32), pltpu.VMEM((16, SLOT, 128), F32)],
        compiler_params=pltpu.CompilerParams(vmem_limit_bytes=VMEM_BYTES),
        name="branches",
    )(*map(on_chip, (centre, *moved, opposite, own_left, own_right, own_terms)), bias, top, bottom)


def coarse_tile(received, weight, pool_weight, bias):
    lane = lax.broadcasted_iota(jnp.int32, (104, 128), 1)
    blocks = [received[source, 0:104].astype(F32) for source in range(16)]
    turned = [pltpu.roll(block, 64, 1) for block in blocks]
    halves = []
    for half in range(2):
        pieces = []
        for source in range(0, 16, 2):
            left = blocks[source] if half == 0 else turned[source]
            right = turned[source + 1] if half == 0 else blocks[source + 1]
            pieces.append(jnp.where(lane < 64, left, right)[0:96])
        halves.append(jnp.concatenate(pieces, axis=1))
    stacked = jnp.concatenate(halves, axis=0).astype(BF)
    low = blocks[0][96:104]
    high = blocks[8][96:104]
    for source in range(1, 8):
        low = low + pltpu.roll(blocks[source][96:104], 16 * source, 1)
        high = high + pltpu.roll(blocks[source + 8][96:104], 16 * source, 1)
    vector = jnp.concatenate([low, high], axis=1).astype(BF)
    constant = jnp.dot(vector, pool_weight, preferred_element_type=F32)[0:1]
    summed = jnp.dot(stacked, weight, preferred_element_type=F32)
    return jnp.maximum(summed + constant + bias[...], 0.0).astype(BF)


def decode_kernel(*refs):
    received, proj, bias, spread, low_own, w1_hbm, b1, w2_hbm, b2 = refs[0:9]
    out, fine, fine_cols, mid, mid_cols, w1, w2, weight, last, low, shift, sems = refs[9:]
    loads = [
        pltpu.make_async_copy(w1_hbm, w1, sems.at[0]),
        pltpu.make_async_copy(w2_hbm, w2, sems.at[1]),
    ]
    small_loads = [
        pltpu.make_async_copy(proj.at[branch], weight.at[:, branch], sems.at[2 + branch])
        for branch in range(4)
    ]
    small_loads.append(pltpu.make_async_copy(proj.at[4], last, sems.at[6]))
    for load in small_loads + loads:
        load.start()
    row_index = lax.axis_index("row_0") * 4 + lax.axis_index("row_1")
    low[...] = low_own[...]
    shift[32:40] = jnp.zeros((8, 128), F32)
    lane = lax.broadcasted_iota(jnp.int32, (32, 128), 1)
    for side in range(2):
        source = row_index - 1 + 2 * side
        inside = (source >= 0) & (source < 16)
        block = received[jnp.clip(source, 0, 15), 104:136].astype(F32)
        for row in range(2):
            values = block if row == 0 else pltpu.roll(block, 64, 1)
            shift[0:32] = jnp.where(inside & (lane < 48), values, 0.0)
            moved = pltpu.roll(shift[2:34], 96, 1)
            front = shift[0:32] + pltpu.roll(shift[1:33], 48, 1)
            front = front + jnp.where(lane >= 96, moved, 0.0)
            filled = jnp.concatenate([front, moved[:, 0:16]], axis=1)
            at = (18 * side + row) * 32
            low[at : at + 32] = filled.astype(BF)
    for load in small_loads:
        load.wait()
    coarse = coarse_tile(
        received, weight[...].reshape(1024, 256), last[...].reshape(256, 256), bias
    )
    fine[0:640] = jnp.dot(spread[...], coarse, preferred_element_type=F32)
    fine[640:656] = jnp.zeros((16, 256), F32)
    for tap in range(3):
        fine_cols[tap] = fine[tap : tap + 640].astype(BF)
    loads[0].wait()
    acc = jnp.zeros((576, 256), F32)
    for row_tap in range(3):
        rows = slice(row_tap * 32, row_tap * 32 + 576)
        for tap in range(3):
            acc = acc + jnp.dot(
                fine_cols[tap, rows], w1[row_tap, tap, 0:256], preferred_element_type=F32
            )
        small = jnp.concatenate([w1[row_tap, tap, 256:304] for tap in range(3)], axis=0)
        acc = acc + jnp.dot(low[rows], small, preferred_element_type=F32)
    at = lax.broadcasted_iota(jnp.int32, (576, 256), 0)
    y = 16 * row_index - 1 + (at >> 5)
    x = 24 * lax.axis_index("col") - 1 + (at & 31)
    inside = (y >= 0) & (y < 2 * MAP_ROWS) & (x >= 0) & (x < 2 * MAP_COLS)
    mid[0:576] = jnp.where(inside, jnp.maximum(acc + b1[...], 0.0), 0.0)
    mid[576:592] = jnp.zeros((16, 256), F32)
    for tap in range(3):
        mid_cols[tap] = mid[tap : tap + 576].astype(BF)
    loads[1].wait()
    acc = jnp.zeros((512, 256), F32)
    for row_tap in range(3):
        for tap in range(3):
            acc = acc + jnp.dot(
                mid_cols[tap, row_tap * 32 : row_tap * 32 + 512],
                w2[row_tap, tap],
                preferred_element_type=F32,
            )
    result = jnp.maximum(acc + b2[...], 0.0).astype(BF).reshape(16, 32, 256)
    out[...] = result[:, 0:24]


def decode(received, proj, bias, spread, low, w1, b1, w2, b2):
    vmem = pl.BlockSpec(memory_space=pltpu.VMEM)
    hbm = pl.BlockSpec(memory_space=pl.ANY)
    return pl.pallas_call(
        decode_kernel,
        out_shape=jax.ShapeDtypeStruct((16, 24, 256), BF),
        in_specs=[vmem, hbm, vmem, vmem, vmem, hbm, vmem, hbm, vmem],
        scratch_shapes=[
            pltpu.VMEM((656, 256), F32),
            pltpu.VMEM((3, 640, 256), BF),
            pltpu.VMEM((592, 256), F32),
            pltpu.VMEM((3, 576, 256), BF),
            pltpu.VMEM(w1.shape, BF),
            pltpu.VMEM(w2.shape, BF),
            pltpu.VMEM((16, 4, 16, 256), BF),
            pltpu.VMEM((16, 16, 256), BF),
            pltpu.VMEM((640, 144), BF),
            pltpu.VMEM((40, 128), F32),
            pltpu.SemaphoreType.DMA((7,)),
        ],
        compiler_params=pltpu.CompilerParams(vmem_limit_bytes=56 * 1024 * 1024),
        name="decode",
    )(on_chip(received), proj, bias, on_chip(spread), on_chip(low), w1, b1, w2, b2)


def spread_kernel(out):
    n = lax.broadcasted_iota(jnp.int32, (640, 192), 0)
    m = lax.broadcasted_iota(jnp.int32, (640, 192), 1)
    col = (m * 683) >> 13
    row_index = lax.axis_index("row_0") * 4 + lax.axis_index("row_1")
    strip = lax.axis_index("col")

    def weights(fine, size, coarse):
        near = fine >> 1
        other = jnp.where((fine & 1) == 1, near + 1, near - 1)
        other = jnp.clip(other, 0, size - 1)
        value = jnp.where(coarse == near, 0.75, 0.0) + jnp.where(coarse == other, 0.25, 0.0)
        return jnp.where((fine >= 0) & (fine < 2 * size), value, 0.0)

    rows = weights(16 * row_index - 2 + (n >> 5), MAP_ROWS, 8 * row_index - 2 + m - 12 * col)
    cols = weights(24 * strip - 2 + (n & 31), MAP_COLS, 12 * strip - 2 + col)
    out[...] = (rows * cols).astype(BF)


def spread_matrix():
    return pl.pallas_call(
        spread_kernel,
        out_shape=pltpu.VMEM((640, 192), BF),
        name="spread",
    )()


def reduce_low(low_level, weight, bias):
    reduced = jnp.dot(
        low_level.reshape(-1, low_level.shape[2]), weight, preferred_element_type=F32
    )
    reduced = jnp.maximum(reduced + bias, 0.0).astype(BF).reshape(16, 24, -1)
    return reduced


def low_columns(wide):
    full = jnp.pad(wide, ((2, 3), (0, 4), (0, 0))).reshape(672, -1)
    return jnp.concatenate([full[tap : tap + 640] for tap in range(3)], axis=1)


def border(rows):
    padded = jnp.pad(rows, ((0, 0), (0, 4), (0, 16)))
    return jnp.concatenate([padded[0], padded[1]], axis=1)


def on_device(
    features,
    low_level,
    point_weight,
    atrous_weight,
    pool_weight,
    aspp_bias,
    proj_weight,
    proj_bias,
    low_weight,
    low_bias,
    conv1_weight,
    conv1_bias,
    conv2_weight,
    conv2_bias,
):
    in_width = features.shape[2]
    tile = jnp.transpose(features, (1, 0, 2))
    reduced = reduce_low(low_level, low_weight, low_bias)
    before = next_to(reduced[:, 22:24], "col", 1)
    after = next_to(reduced[:, 0:2], "col", -1)
    wide = jnp.concatenate([before, reduced, after], axis=1)
    low, top, bottom = low_columns(wide), border(wide[0:2]), border(wide[14:16])
    pieces_a = gather_strip(tile[:6], "row_1", "row_0")
    pieces_b = gather_strip(tile[6:], "row_0", "row_1")
    spread = spread_matrix()
    atrous = jnp.transpose(atrous_weight, (0, 1, 2, 4, 3)).reshape(432, in_width)
    point, pool = point_weight.T, pool_weight.T
    early = early_products(pieces_a[:6] + pieces_b[:6], atrous, point, pool)
    late = pieces_a[6:] + pieces_b[6:]
    centre, *sides, opposite = products(early, late, atrous, point, pool)
    moved = []
    for rate in range(3):
        moved.append(around(sides[2 * rate], "col", rate + 1))
        moved.append(around(sides[2 * rate + 1], "col", -rate - 1))
    across = around(opposite, "col", 4)
    mine = branches(
        centre, moved, across, sides[0], sides[1], opposite, aspp_bias, top, bottom
    )
    received = lax.all_to_all(mine, ROW, split_axis=0, concat_axis=0, tiled=True)
    return decode(
        received,
        proj_weight.reshape(5, 16, 16, 256),
        proj_bias.reshape(1, 256),
        spread,
        low,
        conv1_weight,
        conv1_bias.reshape(1, 256),
        conv2_weight,
        conv2_bias.reshape(1, 256),
    )


def solution(mesh):
    torus = Mesh(
        mesh.devices.reshape(mesh.shape["dp"], 4, 4, mesh.shape["col"]),
        ("dp", "row_0", "row_1", "col"),
    )
    placed = (
        P(DP_ROW, "col", None),
        P(DP_ROW, "col", None),
        P(None, ROW),
        P(None, None, None, None, ROW),
        P(None, ROW),
        P(None, ROW),
        P(),
        P(),
        P(),
        P(),
        P(),
        P(),
        P(),
        P(),
    )
    return jax.shard_map(
        on_device, mesh=torus, in_specs=placed, out_specs=P(DP_ROW, "col", None), check_vma=False
    )
```
